256 devices in a mesh: win: 32 (over x, z), ch: 8 (over y, core).
Axes of the slice: x: 4, y: 4, z: 8, core: 2. Of those that a mesh axis runs over, the one named last changes fastest.
Arguments:
- spectra: bfloat16 [384, 1024, 512], P('win', 'ch'), may hold values from -40 to 40
- sources: int32 [8], replicated, may hold values from 0 to 1023
- valid: int32 [384], P('win'), may hold values from 0 to 1, as said below
Outputs:
- weights: float32 [384, 8, 1024], P('win', None, 'ch')
- beamed: float32 [256, 8, 2, 512], P(('win', 'ch'))
The draws below stay inside these ranges and needn't reach their ends.
Inputs may be any that keep to these rules, and one draw needn't show every extreme that they name: At least one window is valid.
All inputs are finite; a program needn't handle non-finite values.
Results may differ from the reference program's by a relative error of at most 0.0003.
The reference program's roundings to bfloat16 on the way count: a program that leaves them out, or rounds other values in their place, can miss the bound.
Values may be sent and summed in bfloat16 or wider, within the bound.
No kernel may reach another device: no remote copies, remote signals or barrier semaphores. Data moves between devices by JAX's collectives and lax.ppermute only.
A program may use at most 64 MiB of HBM per device.

```python
import math
import jax
import jax.numpy as jnp
from jax import lax

WIN_DEV = 12
S = 8
NCH = 1024
F = 256
L = 256
P_SIZE = 512
ITERS = 3
NWIN = 384


def draw_spectra(key, part):
    subkeys = jax.random.split(jax.random.fold_in(key, 11), 8)
    window_ids = jnp.arange(NWIN, dtype=jnp.float32)
    turning = 0.5 * math.pi * window_ids / NWIN
    first_share = jnp.cos(turning)
    second_share = jnp.sin(turning)
    window_scale = jnp.exp(jax.random.uniform(subkeys[0], (NWIN,), jnp.float32, 0.0, math.log(1.2)))
    channel_scale = jnp.exp(jax.random.uniform(subkeys[1], (NCH,), jnp.float32, 0.0, math.log(2.0)))
    trial_count = NWIN // WIN_DEV + 1
    shift_amount = jax.random.randint(subkeys[6], (), 0, WIN_DEV)
    run_ids = (jnp.arange(NWIN, dtype=jnp.int32) + shift_amount) // WIN_DEV
    states = jax.random.randint(subkeys[7], (trial_count,), 0, 10)
    live_segment_mask = states[run_ids] < 3
    transient_spikes = jnp.where(live_segment_mask, 1.0, 0.2).astype(jnp.float32)
    random_background = jax.random.normal(subkeys[2], (NWIN, NCH, 2 * F), jnp.float32)
    shared_one = jax.random.normal(subkeys[3], (NCH, 2 * F), jnp.float32)
    shared_two = jax.random.normal(subkeys[5], (NCH, 2 * F), jnp.float32)
    consistent_waveform = first_share[:, None, None] * shared_one[None] + second_share[:, None, None] * shared_two[None]
    blend_fractions = transient_spikes[:, None, None] * consistent_waveform + 0.25 * random_background
    values = blend_fractions * window_scale[:, None, None] * channel_scale[None, :, None]
    return jnp.clip(values, -40.0, 40.0).astype(jnp.bfloat16)


def draw_valid(key, part):
    subkeys = jax.random.split(jax.random.fold_in(key, 23), 3)
    block_ids = jnp.arange(NWIN, dtype=jnp.int32) // WIN_DEV
    levels = jax.random.randint(subkeys[0], (NWIN // WIN_DEV,), 0, 4)
    drawn = jax.random.randint(subkeys[1], (NWIN,), 0, 8)
    sparse = levels[block_ids] == 0
    keep = jnp.where(sparse, drawn == 0, drawn < 6)
    chosen = jax.random.randint(subkeys[2], (), 0, NWIN)
    keeper = keep | (jnp.arange(NWIN, dtype=jnp.int32) == chosen)
    return keeper.astype(jnp.int32)


def with_ends(values, key, least, top_value):
    index_at = [jax.random.randint(jax.random.fold_in(key, axis), (), 0, length) for axis, length in enumerate(values.shape)]
    widest = values.shape.index(max(values.shape))
    neighbour = index_at[:widest] + [(index_at[widest] + 1) % values.shape[widest]] + index_at[widest + 1:]
    return values.at[tuple(index_at)].set(least).at[tuple(neighbour)].set(top_value)


def setup_inputs(seed: int = 0) -> dict:
    key_list = jax.random.split(jax.random.key(seed), 4)
    return {
        "spectra": draw_spectra(jax.random.fold_in(key_list[3], 71), 0),
        "sources": with_ends(jax.random.randint(key_list[1], (S,), 0, NCH), jax.random.fold_in(key_list[1], 1), 0, NCH - 1).astype(jnp.int32),
        "valid": draw_valid(jax.random.fold_in(key_list[3], 71), 0),
    }


degrees = 3.0
epsilon = 1e-06

def inverse_table(freq_count, lag_count):
    freq_ids = jnp.arange(freq_count, dtype=jnp.int32)
    delay_indices = jnp.arange(lag_count, dtype=jnp.int32) - lag_count // 2
    phase_ids = jnp.mod(freq_ids[:, None] * delay_indices[None, :], 2 * freq_count)
    angles = 2.0 * math.pi / (2 * freq_count) * phase_ids.astype(jnp.float32)
    factor = 1.0 / math.sqrt(freq_count)
    return jnp.concatenate([jnp.cos(angles) * factor, -jnp.sin(angles) * factor], axis=0).astype(jnp.bfloat16)

def cross_rows(source_rows, channel_rows):
    freq_count = channel_rows.shape[-1] // 2
    source_f = source_rows.astype(jnp.float32)
    channel_f = channel_rows.astype(jnp.float32)
    source_real = source_f[:, None, :freq_count]
    source_imag = source_f[:, None, freq_count:]
    real_channel_rows = channel_f[None, :, :freq_count]
    channel_imag = channel_f[None, :, freq_count:]
    real_part = source_real * real_channel_rows + source_imag * channel_imag
    imag_part = source_imag * real_channel_rows - source_real * channel_imag
    return jnp.concatenate([real_part, imag_part], axis=-1).astype(jnp.bfloat16)

def correlate(paired, inverse):
    crossed = cross_rows(paired[0], paired[1])
    flattened_rows = crossed.reshape(-1, crossed.shape[-1]).astype(jnp.float32)
    product = jnp.dot(flattened_rows, inverse.astype(jnp.float32), preferred_element_type=jnp.float32)
    return product.astype(jnp.bfloat16).reshape(crossed.shape[0], crossed.shape[1], inverse.shape[1])

def forward_table(first_row, row_count, freq_count, lag_count):
    freq_ids = first_row + jnp.arange(row_count, dtype=jnp.int32)
    delay_indices = jnp.arange(lag_count, dtype=jnp.int32) - lag_count // 2
    phase_ids = jnp.mod(freq_ids[:, None] * delay_indices[None, :], 2 * freq_count)
    angles = 2.0 * math.pi / (2 * freq_count) * phase_ids.astype(jnp.float32)
    factor = 1.0 / math.sqrt(lag_count)
    return jnp.stack([jnp.cos(angles) * factor, -jnp.sin(angles) * factor], axis=1)

def transform(stacked, first_row, row_count, freq_count):
    table_rows = forward_table(first_row, row_count, freq_count, stacked.shape[-1])
    return jnp.einsum('kal,scl->kasc', table_rows, stacked, precision=lax.Precision.HIGHEST)

def beam_one(freq_id, spectrum, freq_count, slow_count, beam_gain):
    chan_count = spectrum.shape[-1]
    chan_ids = jnp.arange(chan_count, dtype=jnp.int32)
    slow_ids = jnp.arange(slow_count, dtype=jnp.int32) - slow_count // 2
    modulus = 4 * freq_count * slow_count
    phase_ids = jnp.mod((freq_id * chan_ids)[:, None] * slow_ids[None, :], modulus)
    angles = 2.0 * math.pi / modulus * phase_ids.astype(jnp.float32)
    cosines = jnp.cos(angles)
    sines = jnp.sin(angles)
    highest = lax.Precision.HIGHEST
    beam_cosine_part = jnp.dot(spectrum[0], cosines, precision=highest, preferred_element_type=jnp.float32) - jnp.dot(spectrum[1], sines, precision=highest, preferred_element_type=jnp.float32)
    imag_beam = jnp.dot(spectrum[0], sines, precision=highest, preferred_element_type=jnp.float32) + jnp.dot(spectrum[1], cosines, precision=highest, preferred_element_type=jnp.float32)
    return jnp.stack([beam_cosine_part, imag_beam], axis=1) * beam_gain

def reference(spectra, sources, valid):
    freq_count = spectra.shape[-1] // 2
    window_total = spectra.shape[0]
    inverse = inverse_table(freq_count, L)
    source_spectra = spectra[:, sources, :]
    correlations = lax.map(lambda paired: correlate(paired, inverse), (source_spectra, spectra))
    by_source = jnp.moveaxis(correlations, 1, 0)
    window_mask = valid.astype(jnp.float32)
    valid_count = jnp.sum(window_mask)

    def weighted_stack(weights):

        def one_source(paired):
            row_weights, source_corr = paired
            numer = lax.optimization_barrier(jnp.sum(row_weights[:, :, None] * source_corr.astype(jnp.float32), axis=0))
            return numer / lax.optimization_barrier(jnp.sum(row_weights, axis=0))[:, None]
        return lax.map(one_source, (weights, by_source))

    def spreads(stacked):

        def one_source(paired):
            source_stack, source_corr = paired
            differ = source_corr.astype(jnp.float32) - source_stack[None]
            return lax.optimization_barrier(jnp.mean(differ * differ, axis=-1))
        return lax.map(one_source, (stacked, by_source))
    weights = jnp.broadcast_to(window_mask[None, :, None], (S, window_total, NCH))
    stacked = weighted_stack(weights)
    for iteration in range(ITERS):
        residual_sq = spreads(stacked)
        spread_sq = jnp.sum(window_mask[None, :, None] * residual_sq) / (S * NCH * valid_count) + epsilon
        weights = window_mask[None, :, None] * (degrees + 1.0) / (degrees + residual_sq / spread_sq)
        stacked = weighted_stack(weights)
    spectrum = transform(stacked, 0, freq_count, freq_count)
    beam_gain = NCH ** (-0.5)
    beamed = lax.map(lambda paired: beam_one(paired[0], paired[1], freq_count, P_SIZE, beam_gain), (jnp.arange(freq_count, dtype=jnp.int32), spectrum))
    return (jnp.moveaxis(weights, 0, 1), beamed)
```

```python
import math

import jax
import jax.numpy as jnp
import numpy as np
from jax import lax
from jax.experimental import pallas as pl
from jax.experimental.pallas import tpu as pltpu
from jax.sharding import PartitionSpec as P

L = 256
P_SIZE = 512
ITERS = 3
Q = 4
LANES = 128

degrees = 3.0
epsilon = 1e-06
HIGHEST = lax.Precision.HIGHEST
NT = (((1,), (1,)), ((), ()))
TN = (((0,), (0,)), ((), ()))


def tables(freq_count, lag_count):
    freq_ids = np.arange(freq_count, dtype=np.int64)
    delays = np.arange(lag_count, dtype=np.int64) - lag_count // 2
    phase_ids = np.mod(freq_ids[:, None] * delays[None, :], 2 * freq_count)
    angles = np.float32(2.0 * math.pi / (2 * freq_count)) * phase_ids.astype(np.float32)
    cosines = np.cos(angles.astype(np.float64)).astype(np.float32)
    sines = np.sin(angles.astype(np.float64)).astype(np.float32)
    inverse_factor = np.float32(1.0 / math.sqrt(freq_count))
    forward_factor = np.float32(1.0 / math.sqrt(lag_count))
    inverse = np.concatenate([cosines * inverse_factor, -sines * inverse_factor], axis=0)
    forward = np.concatenate([cosines * forward_factor, -sines * forward_factor], axis=0)
    return np.ascontiguousarray(inverse.T), forward


def pick_kernel(ids_ref, x_ref, o_ref):
    rows, chan_dev = x_ref.shape[0], 128
    win_dev = rows // chan_dev
    row = lax.broadcasted_iota(jnp.int32, (16, rows), 0)
    col = lax.broadcasted_iota(jnp.int32, (16, rows), 1)
    shift = ids_ref[o_ref.shape[0]]
    blocks = []
    for s in range(o_ref.shape[0]):
        base = ids_ref[s] - shift
        base = jnp.where((base >= 0) & (base < chan_dev), base, -(1 << 20))
        hit = (col == row * chan_dev + base) & (row < win_dev)
        blocks.append(jnp.where(hit, 1.0, 0.0))
    picker = jnp.concatenate(blocks, axis=0).astype(jnp.bfloat16)
    picked = jnp.dot(picker, x_ref[...], preferred_element_type=jnp.float32)
    o_ref[...] = picked.astype(jnp.bfloat16).reshape(o_ref.shape)


def pack_kernel(x_ref, o_ref):
    row = lax.broadcasted_iota(jnp.int32, (512, 512), 0)
    col = lax.broadcasted_iota(jnp.int32, (512, 512), 1)
    src = (row % 4) * 128 + (row // 16) * 4 + (row // 4) % 4
    perm = jnp.where(col == src, 1.0, 0.0).astype(jnp.bfloat16)
    for t in range(o_ref.shape[1] // 16):
        got = jnp.dot(perm, x_ref[t * 512:(t + 1) * 512, :], preferred_element_type=jnp.float32)
        o_ref[:, t * 16:(t + 1) * 16, :] = got.astype(jnp.bfloat16).reshape(
            o_ref.shape[0], 16, x_ref.shape[1]
        )


def same_channel():
    a = lax.broadcasted_iota(jnp.int32, (LANES, LANES), 0)
    b = lax.broadcasted_iota(jnp.int32, (LANES, LANES), 1)
    return jnp.where((a // 4) % 4 == (b // 4) % 4, 1.0, 0.0)


LAG_CHUNK = 64


def weighted_stack(c_ref, weights, acc_ref):
    blocks = weights.shape[0]
    for k in range(L // LAG_CHUNK):
        lags = slice(k * LAG_CHUNK, (k + 1) * LAG_CHUNK)
        acc = jnp.zeros((LAG_CHUNK, LANES), jnp.float32)
        for b in range(blocks):
            acc += weights[b:b + 1, :] * c_ref[0, lags, b * LANES:(b + 1) * LANES].astype(jnp.float32)
        acc_ref[lags, :] = acc
    group = same_channel()
    numer = jnp.dot(acc_ref[...], group, precision=HIGHEST, preferred_element_type=jnp.float32)
    weight_sum = jnp.broadcast_to(jnp.sum(weights, axis=0, keepdims=True), (8, LANES))
    denom = jnp.dot(weight_sum, group, precision=HIGHEST, preferred_element_type=jnp.float32)
    return numer / denom[0:1, :]


def residuals(c_ref, stack_ref, r_ref):
    blocks = r_ref.shape[1]
    for b in range(blocks):
        total = jnp.zeros((8, LANES), jnp.float32)
        for k in range(L // LAG_CHUNK):
            lags = slice(k * LAG_CHUNK, (k + 1) * LAG_CHUNK)
            d = c_ref[0, lags, b * LANES:(b + 1) * LANES].astype(jnp.float32) - stack_ref[lags, :]
            total += jnp.sum((d * d).reshape(LAG_CHUNK // 8, 8, LANES), axis=0)
        r_ref[0, b:b + 1, :] = jnp.sum(total, axis=0, keepdims=True) * (1.0 / L)


def finish_residuals(step, last, mask_ref, c_ref, acc_ref, r_ref, part_ref, sum_ref):
    residuals(c_ref, acc_ref, r_ref)
    part = jnp.sum(mask_ref[...] * r_ref[0], axis=0, keepdims=True)

    @pl.when(step == 0)
    def _():
        sum_ref[...] = jnp.zeros_like(sum_ref)

    sum_ref[...] += jnp.broadcast_to(part, sum_ref.shape)

    @pl.when(step == last)
    def _():
        part_ref[...] = jnp.broadcast_to(sum_ref[0:1, :], part_ref.shape)


def correlate_kernel(
    ids_ref, a_ref, x_ref, y_ref, inv_ref, mask_ref, c_ref, r_ref, part_ref, cross_ref, acc_ref, sum_ref
):
    step = pl.program_id(0)
    freq_count = a_ref.shape[1] // 2
    low = lax.broadcasted_iota(jnp.int32, (8, a_ref.shape[1]), 0) < 4

    def fill(s_ref):
        def one(j, carry):
            src = s_ref[0, j].astype(jnp.float32)
            first, last = src[0:8], src[8:16]
            turned = pltpu.roll(first, 4, 0)
            tiles = (
                jnp.where(low, first, turned),
                jnp.where(low, turned, first),
                jnp.where(low, last, pltpu.roll(last, 4, 0)),
            )
            for t in range(3):
                rows = pl.ds(pl.multiple_of(j * 48 + t * 16, 16), 16)
                chan = a_ref[rows, :].astype(jnp.float32)
                tile = jnp.concatenate([tiles[t], tiles[t]], axis=0)
                a, b = tile[:, :freq_count], tile[:, freq_count:]
                u, v = chan[:, :freq_count], chan[:, freq_count:]
                cross_ref[rows, :freq_count] = (a * u + b * v).astype(jnp.bfloat16)
                cross_ref[rows, freq_count:] = (b * u - a * v).astype(jnp.bfloat16)
            return carry

        lax.fori_loop(0, s_ref.shape[1], one, 0, unroll=2)

    @pl.when(step < 4)
    def _():
        fill(x_ref)

    @pl.when(step >= 4)
    def _():
        fill(y_ref)

    for n in range(a_ref.shape[0] // 256):
        got = lax.dot_general(
            inv_ref[...], cross_ref[n * 256:(n + 1) * 256, :], NT, preferred_element_type=jnp.float32
        )
        c_ref[0, :, n * 256:(n + 1) * 256] = got.astype(jnp.bfloat16)
    acc_ref[...] = weighted_stack(c_ref, mask_ref[...], acc_ref)
    finish_residuals(step, pl.num_programs(0) - 1, mask_ref, c_ref, acc_ref, r_ref, part_ref, sum_ref)


def next_weights(total, mask, r, pairs):
    spread = total / (pairs * jnp.sum(mask) * (1.0 / Q)) + epsilon
    return mask * (degrees + 1.0) / (degrees + r / spread)


def iterate_kernel(pairs, all_ref, mask_ref, r_in_ref, c_ref, r_ref, part_ref, acc_ref, sum_ref):
    step = pl.program_id(0)
    weights = next_weights(jnp.sum(all_ref[...]), mask_ref[...], r_in_ref[0], pairs)
    acc_ref[...] = weighted_stack(c_ref, weights, acc_ref)
    finish_residuals(step, pl.num_programs(0) - 1, mask_ref, c_ref, acc_ref, r_ref, part_ref, sum_ref)


def spectrum_kernel(pairs, all_ref, mask_ref, r_in_ref, c_ref, table_ref, o_ref, acc_ref, all_stack_ref):
    step = pl.program_id(0)
    weights = next_weights(jnp.sum(all_ref[...]), mask_ref[...], r_in_ref[0], pairs)
    stack = weighted_stack(c_ref, weights, acc_ref)
    lane = lax.broadcasted_iota(jnp.int32, (L, LANES), 1)
    mine = jnp.where(lane // 16 == step, stack, 0.0)

    @pl.when(step == 0)
    def _():
        all_stack_ref[...] = mine

    @pl.when(step > 0)
    def _():
        all_stack_ref[...] += mine

    @pl.when(step == pl.num_programs(0) - 1)
    def _():
        both = jnp.dot(
            table_ref[...], all_stack_ref[...], precision=HIGHEST, preferred_element_type=jnp.float32
        )
        freq_count = table_ref.shape[0] // 2
        part = lax.broadcasted_iota(jnp.int32, (freq_count, LANES), 1) % 4
        o_ref[...] = jnp.where(part == 0, both[:freq_count], jnp.where(part == 1, both[freq_count:], 0.0))


def beam_kernel(gain, x_ref, cos_ref, sin_ref, fine_cos_ref, fine_sin_ref, o_ref):
    x = x_ref[...]
    yc = lax.dot_general(x, cos_ref[...], TN, precision=HIGHEST, preferred_element_type=jnp.float32)
    ys = lax.dot_general(x, sin_ref[...], TN, precision=HIGHEST, preferred_element_type=jnp.float32)
    c, s = fine_cos_ref[...], fine_sin_ref[...]
    u = yc * c - ys * s
    v = ys * c + yc * s
    rows = o_ref.shape[0]
    out = lax.broadcasted_iota(jnp.int32, (rows, LANES), 0)
    lane = lax.broadcasted_iota(jnp.int32, (rows, LANES), 1)
    same = lane // 16 == out // 2
    imag, part = out % 2, lane % 4
    pick_u = jnp.where(same & (part == imag), 1.0, 0.0)
    pick_v = jnp.where(same & (part == 0) & (imag == 1), 1.0, 0.0) - jnp.where(
        same & (part == 1) & (imag == 0), 1.0, 0.0
    )
    beams = jnp.dot(pick_u, u, precision=HIGHEST, preferred_element_type=jnp.float32) + jnp.dot(
        pick_v, v, precision=HIGHEST, preferred_element_type=jnp.float32
    )
    o_ref[...] = beams * gain


def cos_sin(freq_id, chan_ids, slow_count, modulus):
    slow_ids = jnp.arange(slow_count, dtype=jnp.int32) - slow_count // 2
    phase_ids = jnp.mod((freq_id * chan_ids)[:, None] * slow_ids[None, :], modulus)
    angles = 2.0 * math.pi / modulus * phase_ids.astype(jnp.float32)
    return jnp.cos(angles), jnp.sin(angles)


def full(shape):
    return pl.BlockSpec(shape, lambda *_: (0,) * len(shape))


def by_source(shape):
    return pl.BlockSpec((1,) + shape, lambda s, *_: (s,) + (0,) * len(shape))


def body(spectra, sources, valid):
    win_dev, chan_dev, width = spectra.shape
    freq_count = width // 2
    source_total = sources.shape[0]
    n_win = lax.axis_size("win")
    n_ch = lax.axis_size("ch")
    n_all = n_win * n_ch
    chans = chan_dev * n_ch
    pairs = float(source_total * chans)
    ch = lax.axis_index("ch")
    y, core = ch // 2, ch % 2
    inverse_np, forward_np = tables(freq_count, L)
    flat = spectra.reshape(win_dev * chan_dev, width)
    rows_dev = win_dev * Q
    rows = n_win * rows_dev
    blocks = rows // LANES

    ids = jnp.concatenate([sources.astype(jnp.int32), (ch * chan_dev).astype(jnp.int32)[None]])
    picked = pl.pallas_call(
        pick_kernel,
        grid_spec=pltpu.PrefetchScalarGridSpec(
            num_scalar_prefetch=1,
            grid=(1,),
            in_specs=[full(flat.shape)],
            out_specs=full((source_total, 16, width)),
        ),
        out_shape=jax.ShapeDtypeStruct((source_total, 16, width), jnp.bfloat16),
        name="pick",
    )(ids, flat)
    got = lax.all_to_all(picked, "ch", 0, 0, tiled=True)
    own = jnp.sum(got.astype(jnp.float32), axis=0)
    mask_row = jnp.pad(valid.astype(jnp.float32), (0, width - win_dev))
    own = jnp.where(jnp.arange(16)[:, None] == win_dev, mask_row[None], own).astype(jnp.bfloat16)
    own = lax.all_to_all(jnp.broadcast_to(own[None], (n_win, 16, width)), "win", 0, 0, tiled=True)

    def turn(d):
        return [(i * 2 + c, ((i + d) % 4) * 2 + c) for i in range(n_ch // 2) for c in range(2)]

    mine = jnp.stack([own] + [lax.ppermute(own, "ch", turn(d)) for d in (1, 2, 3)])
    theirs = lax.ppermute(mine, "ch", [(i, i ^ 1) for i in range(n_ch)])
    steps = jnp.arange(4, dtype=jnp.int32)
    slot_y = 2 * ((y - steps) % 4)
    slots = jnp.concatenate([slot_y + core, slot_y + 1 - core]).astype(jnp.int32)
    mask = own[:, win_dev, :win_dev].astype(jnp.float32).reshape(n_win, win_dev // 4, 1, 4)
    mask = jnp.broadcast_to(mask, (n_win, win_dev // 4, Q, 4)).reshape(blocks, LANES)

    packed = pl.pallas_call(
        pack_kernel,
        out_shape=jax.ShapeDtypeStruct((n_win, rows_dev, width), jnp.bfloat16),
        name="pack",
    )(flat)
    moved = lax.all_to_all(packed, "win", 0, 0, tiled=True).reshape(rows, width)

    corr_shape = jax.ShapeDtypeStruct((source_total, L, rows), jnp.bfloat16)
    r_shape = jax.ShapeDtypeStruct((source_total, blocks, LANES), jnp.float32)
    part_shape = jax.ShapeDtypeStruct((n_all, LANES), jnp.float32)
    slot = lambda s, ids_ref: (ids_ref[s], 0, 0)
    corr, r, part = pl.pallas_call(
        correlate_kernel,
        grid_spec=pltpu.PrefetchScalarGridSpec(
            num_scalar_prefetch=1,
            grid=(source_total,),
            in_specs=[
                full((rows, width)),
                pl.BlockSpec((1, n_win, 16, width), lambda s, _: (jnp.minimum(s, 3), 0, 0, 0)),
                pl.BlockSpec((1, n_win, 16, width), lambda s, _: (jnp.maximum(s - 4, 0), 0, 0, 0)),
                full((L, width)),
                full((blocks, LANES)),
            ],
            out_specs=[
                pl.BlockSpec((1, L, rows), slot),
                pl.BlockSpec((1, blocks, LANES), slot),
                full((n_all, LANES)),
            ],
            scratch_shapes=[
                pltpu.VMEM((rows, width), jnp.bfloat16),
                pltpu.VMEM((L, LANES), jnp.float32),
                pltpu.VMEM((8, LANES), jnp.float32),
            ],
        ),
        out_shape=[corr_shape, r_shape, part_shape],
        name="correlate",
    )(slots, moved, mine, theirs, jnp.asarray(inverse_np, jnp.bfloat16), mask)

    for _ in range(ITERS - 1):
        parts = lax.all_to_all(part, ("win", "ch"), 0, 0, tiled=True)
        r, part = pl.pallas_call(
            lambda *refs: iterate_kernel(pairs, *refs),
            grid=(source_total,),
            in_specs=[
                full((n_all, LANES)),
                full((blocks, LANES)),
                by_source((blocks, LANES)),
                by_source((L, rows)),
            ],
            out_specs=[by_source((blocks, LANES)), full((n_all, LANES))],
            out_shape=[r_shape, part_shape],
            scratch_shapes=[pltpu.VMEM((L, LANES), jnp.float32), pltpu.VMEM((8, LANES), jnp.float32)],
            name="iterate",
        )(parts, mask, r, corr)

    sums = jnp.sum(lax.all_to_all(part[:n_ch], "ch", 0, 0, tiled=True), axis=(0, 1))
    home = jnp.swapaxes(r.reshape(source_total, n_win, rows_dev), 0, 1)
    tail = jnp.broadcast_to(sums, (n_win, source_total, LANES - rows_dev))
    back = lax.all_to_all(jnp.concatenate([home, tail], axis=2), "win", 0, 0, tiled=True)
    total = jnp.sum(back[:, 0, rows_dev])
    parts = jnp.zeros((8, LANES), jnp.float32).at[0, 0].set(total)

    spectrum = pl.pallas_call(
        lambda *refs: spectrum_kernel(pairs, *refs),
        grid=(source_total,),
        in_specs=[
            full((8, LANES)),
            full((blocks, LANES)),
            by_source((blocks, LANES)),
            by_source((L, rows)),
            full(forward_np.shape),
        ],
        out_specs=full((freq_count, LANES)),
        out_shape=jax.ShapeDtypeStruct((freq_count, LANES), jnp.float32),
        scratch_shapes=[pltpu.VMEM((L, LANES), jnp.float32), pltpu.VMEM((L, LANES), jnp.float32)],
        name="spectrum",
    )(parts, mask, r, corr, jnp.asarray(forward_np))
    pieces = lax.all_to_all(spectrum, ("win", "ch"), 0, 0, tiled=True)

    freq_id = lax.axis_index("win") * n_ch + ch
    modulus = 4 * freq_count * P_SIZE
    device = jnp.arange(n_all, dtype=jnp.int32)
    coarse = (device % n_ch) * chan_dev + (device // n_ch) * Q
    cosines, sines = cos_sin(freq_id, coarse, P_SIZE, modulus)
    fine_cos, fine_sin = cos_sin(freq_id, (jnp.arange(LANES, dtype=jnp.int32) // 4) % Q, P_SIZE, modulus)
    beamed = pl.pallas_call(
        lambda *refs: beam_kernel(chans ** (-0.5), *refs),
        out_shape=jax.ShapeDtypeStruct((source_total * 2, P_SIZE), jnp.float32),
        name="beam",
    )(pieces, cosines, sines, fine_cos, fine_sin)

    window_count = jnp.sum(mask) * (1.0 / Q)
    spread_sq = total / (pairs * window_count) + epsilon
    mine_mask = valid.astype(jnp.float32)
    residual = back[:, :, :rows_dev].reshape(n_win, source_total, win_dev // 4, Q, 4)
    residual = residual.transpose(2, 4, 1, 0, 3).reshape(win_dev, source_total, chan_dev)
    weights = mine_mask[:, None, None] * (degrees + 1.0) / (degrees + residual / spread_sq)
    return (weights, beamed.reshape(1, source_total, 2, P_SIZE))


def solution(mesh):
    return jax.shard_map(
        body,
        mesh=mesh,
        in_specs=(P("win", "ch", None), P(), P("win")),
        out_specs=(P("win", None, "ch"), P(("win", "ch"), None, None, None)),
        check_vma=False,
    )
```

```python
import math

import jax
import jax.numpy as jnp
import numpy as np
from jax import lax
from jax.experimental import pallas as pl
from jax.experimental.pallas import tpu as pltpu
from jax.sharding import PartitionSpec as P

L = 256
P_SIZE = 512
ITERS = 3
Q = 4
LANES = 128
PARAMS = pltpu.CompilerParams(vmem_limit_bytes=20 << 20)
BIG = pltpu.CompilerParams(vmem_limit_bytes=59 << 20)

degrees = 3.0
epsilon = 1e-06
HIGHEST = lax.Precision.HIGHEST
NT = (((1,), (1,)), ((), ()))
TN = (((0,), (0,)), ((), ()))


def tables(freq_count, lag_count):
    freq_ids = np.arange(freq_count, dtype=np.int64)
    delays = np.arange(lag_count, dtype=np.int64) - lag_count // 2
    phase_ids = np.mod(freq_ids[:, None] * delays[None, :], 2 * freq_count)
    angles = np.float32(2.0 * math.pi / (2 * freq_count)) * phase_ids.astype(np.float32)
    cosines = np.cos(angles.astype(np.float64)).astype(np.float32)
    sines = np.sin(angles.astype(np.float64)).astype(np.float32)
    inverse_factor = np.float32(1.0 / math.sqrt(freq_count))
    forward_factor = np.float32(1.0 / math.sqrt(lag_count))
    inverse = np.concatenate([cosines * inverse_factor, -sines * inverse_factor], axis=0)
    forward = np.concatenate([cosines * forward_factor, -sines * forward_factor], axis=0)
    return np.ascontiguousarray(inverse.T), forward


def pick_kernel(sources_ref, x_ref, o_ref):
    rows, count = x_ref.shape[0], o_ref.shape[0]
    chan_dev = 128
    row = lax.broadcasted_iota(jnp.int32, (24, rows), 0)
    col = lax.broadcasted_iota(jnp.int32, (24, rows), 1)
    window = (row // 8) * 4 + row % 4
    shift = lax.axis_index("ch") * chan_dev
    blocks = []
    for s in range(count):
        base = sources_ref[s] - shift
        base = jnp.where((base >= 0) & (base < chan_dev), base, -(1 << 20))
        blocks.append(jnp.where(col == window * chan_dev + base, 1.0, 0.0))
    picker = jnp.concatenate(blocks, axis=0).astype(jnp.bfloat16)
    picked = jnp.dot(picker, x_ref[...], preferred_element_type=jnp.float32).reshape(count, 24, 512)
    low = lax.broadcasted_iota(jnp.int32, (8, LANES), 0) < 4
    for s in range(count):
        for t in range(3):
            tile = picked[s, t * 8:(t + 1) * 8, :]
            pair = [
                jnp.where(low, tile[:, p * 256:p * 256 + 128], tile[:, p * 256 + 128:p * 256 + 256])
                for p in range(2)
            ]
            o_ref[s, t * 16:(t + 1) * 16, :] = jnp.concatenate(pair, axis=0).astype(jnp.bfloat16)


def own_kernel(x_ref, mask_ref, o_ref):
    total = x_ref[0].astype(jnp.float32)
    for g in range(1, x_ref.shape[0]):
        total += x_ref[g].astype(jnp.float32)
    rows = total.shape[0]
    masks = jnp.broadcast_to(mask_ref[...], (8, LANES))
    block = jnp.concatenate([total, masks], axis=0).astype(jnp.bfloat16)
    for j in range(o_ref.shape[0]):
        o_ref[j] = block


def pack_kernel(x_ref, o_ref):
    row = lax.broadcasted_iota(jnp.int32, (512, 512), 0)
    col = lax.broadcasted_iota(jnp.int32, (512, 512), 1)
    src = (row % 4) * 128 + (row // 16) * 4 + (row // 4) % 4
    perm = jnp.where(col == src, 1.0, 0.0).astype(jnp.bfloat16)
    for t in range(o_ref.shape[1] // 16):
        got = jnp.dot(perm, x_ref[t * 512:(t + 1) * 512, :], preferred_element_type=jnp.float32)
        o_ref[:, t * 16:(t + 1) * 16, :] = got.astype(jnp.bfloat16).reshape(
            o_ref.shape[0], 16, x_ref.shape[1]
        )


LAG_CHUNK = 64


def three_terms(x):
    high = x.astype(jnp.bfloat16)
    rest = x - high.astype(jnp.float32)
    middle = rest.astype(jnp.bfloat16)
    low = (rest - middle.astype(jnp.float32)).astype(jnp.bfloat16)
    return high, middle, low


def same_channel():
    a = lax.broadcasted_iota(jnp.int32, (3 * LANES, LANES), 0)
    b = lax.broadcasted_iota(jnp.int32, (3 * LANES, LANES), 1)
    return jnp.where((a // 4) % 4 == (b // 4) % 4, 1.0, 0.0).astype(jnp.bfloat16)


def weighted_sums(c_ref, s, w_rows, terms_ref):
    weights = [w_rows[b:b + 1, :] for b in range(w_rows.shape[0])]
    for k in range(L // LAG_CHUNK):
        lags = slice(k * LAG_CHUNK, (k + 1) * LAG_CHUNK)
        acc = jnp.zeros((LAG_CHUNK, LANES), jnp.float32)
        for b, w in enumerate(weights):
            acc += w * c_ref[s, lags, b * LANES:(b + 1) * LANES].astype(jnp.float32)
        for i, term in enumerate(three_terms(acc)):
            terms_ref[s, lags, i * LANES:(i + 1) * LANES] = term
    weight_sum = jnp.broadcast_to(jnp.sum(w_rows[...], axis=0, keepdims=True), (16, LANES))
    for i, term in enumerate(three_terms(weight_sum)):
        terms_ref[s, L:L + 16, i * LANES:(i + 1) * LANES] = term


def finish_stacks(terms_ref, stack_ref):
    group = same_channel()
    for s in range(terms_ref.shape[0]):
        sums = jnp.dot(terms_ref[s], group, preferred_element_type=jnp.float32)
        stack_ref[s] = sums[:L] * (1.0 / sums[L:L + 1])


def residuals(c_ref, s, stack_ref, r_ref):
    for b in range(r_ref.shape[1]):
        total = jnp.zeros((8, LANES), jnp.float32)
        for k in range(L // LAG_CHUNK):
            lags = slice(k * LAG_CHUNK, (k + 1) * LAG_CHUNK)
            d = c_ref[s, lags, b * LANES:(b + 1) * LANES].astype(jnp.float32) - stack_ref[s, lags, :]
            total += jnp.sum((d * d).reshape(LAG_CHUNK // 8, 8, LANES), axis=0)
        r_ref[s, b:b + 1, :] = jnp.sum(total, axis=0, keepdims=True) * (1.0 / L)


def masked_sum(mask_ref, r_ref):
    return jnp.sum(mask_ref[...][None] * r_ref[...])


def correlate_kernel(
    ids_ref, a_ref, x_ref, inv_ref, c_hbm, r_ref, part_ref, mask_ref, even_ref, odd_ref, c_ref, terms_ref, stack_ref, sems
):
    n_win, rows = x_ref.shape[1], a_ref.shape[0]
    half = a_ref.shape[1] // 2
    rows_dev = rows // n_win
    low = lax.broadcasted_iota(jnp.int32, (8, LANES), 0) < 4

    lane = lax.broadcasted_iota(jnp.int32, (8, LANES), 1)
    pieces = [jnp.zeros((8, LANES), jnp.float32) for _ in range(rows // LANES)]
    for j in range(n_win):
        row = x_ref[0, j, 48:56, :].astype(jnp.float32)
        b, off = divmod(j * rows_dev, LANES)
        turned = pltpu.roll(row, off, 1) if off else row
        end = off + rows_dev
        pieces[b] = jnp.where((lane >= off) & (lane < end), turned, pieces[b])
        if end > LANES:
            pieces[b + 1] = jnp.where(lane < end - LANES, turned, pieces[b + 1])
    for b, piece in enumerate(pieces):
        mask_ref[b:b + 1, :] = piece[0:1, :]

    count, half_rows = c_ref.shape[0], rows // 2
    half_win = n_win // 2

    def fill(cross_ref, k, side):
        for j in range(half_win):
            for t in range(3):
                quarters = []
                for p in range(2):
                    at = t * 16 + p * 8
                    tile = x_ref[k, side * half_win + j, at:at + 8, :].astype(jnp.float32)
                    turned = pltpu.roll(tile, 4, 0)
                    quarters += [jnp.where(low, tile, turned), jnp.where(low, turned, tile)]
                at = slice(j * rows_dev + t * 16, j * rows_dev + t * 16 + 16)
                src = slice(at.start + side * half_rows, at.stop + side * half_rows)
                for i in range(2):
                    a = jnp.concatenate([quarters[i]] * 2, axis=0)
                    b = jnp.concatenate([quarters[2 + i]] * 2, axis=0)
                    first = slice(i * LANES, (i + 1) * LANES)
                    second = slice(half + i * LANES, half + (i + 1) * LANES)
                    u = a_ref[src, first].astype(jnp.float32)
                    v = a_ref[src, second].astype(jnp.float32)
                    cross_ref[at, first] = (a * u + b * v).astype(jnp.bfloat16)
                    cross_ref[at, second] = (b * u - a * v).astype(jnp.bfloat16)

    def correlate(cross_ref, s, side):
        for n in range(half_rows // 256):
            got = lax.dot_general(
                inv_ref[...], cross_ref[n * 256:(n + 1) * 256, :], NT, preferred_element_type=jnp.float32
            )
            at = side * half_rows + n * 256
            c_ref[s, :, at:at + 256] = got.astype(jnp.bfloat16)

    fill(even_ref, 0, 0)

    def slot(k, carry):
        s = ids_ref[k]
        correlate(even_ref, s, 0)
        fill(odd_ref, k, 1)
        correlate(odd_ref, s, 1)
        fill(even_ref, jnp.minimum(k + 1, count - 1), 0)
        pltpu.make_async_copy(c_ref.at[s], c_hbm.at[s], sems.at[s]).start()
        weighted_sums(c_ref, s, mask_ref, terms_ref)
        return carry

    lax.fori_loop(0, count, slot, 0)
    finish_stacks(terms_ref, stack_ref)

    def last(s, carry):
        residuals(c_ref, s, stack_ref, r_ref)
        return carry

    lax.fori_loop(0, count, last, 0)
    part_ref[...] = jnp.full(part_ref.shape, masked_sum(mask_ref, r_ref), jnp.float32)
    for s in range(c_ref.shape[0]):
        pltpu.make_async_copy(c_ref.at[s], c_hbm.at[s], sems.at[s]).wait()


def set_weights(pairs, total, mask_ref, r_ref, w_ref):
    mask = mask_ref[...]
    spread = total / (pairs * jnp.sum(mask) * (1.0 / Q)) + epsilon
    w_ref[...] = mask[None] * (degrees + 1.0) / (degrees + r_ref[...] / spread)


def start_all(c_hbm, c_ref, sems):
    for s in range(c_ref.shape[0]):
        pltpu.make_async_copy(c_hbm.at[s], c_ref.at[s], sems.at[s]).start()


def iterate_core(pairs, all_ref, mask_ref, r_in_ref, c_hbm, r_ref, c_ref, w_ref, terms_ref, stack_ref, sems):
    start_all(c_hbm, c_ref, sems)
    set_weights(pairs, jnp.sum(all_ref[...]) * (1.0 / LANES), mask_ref, r_in_ref, w_ref)

    def one(s, carry):
        pltpu.make_async_copy(c_hbm.at[s], c_ref.at[s], sems.at[s]).wait()
        weighted_sums(c_ref, s, w_ref.at[s], terms_ref)
        return carry

    lax.fori_loop(0, c_ref.shape[0], one, 0)
    finish_stacks(terms_ref, stack_ref)

    def last(s, carry):
        residuals(c_ref, s, stack_ref, r_ref)
        return carry

    lax.fori_loop(0, c_ref.shape[0], last, 0)


def iterate_kernel(pairs, all_ref, mask_ref, r_in_ref, c_hbm, r_ref, part_ref, c_ref, w_ref, terms_ref, stack_ref, sems):
    iterate_core(pairs, all_ref, mask_ref, r_in_ref, c_hbm, r_ref, c_ref, w_ref, terms_ref, stack_ref, sems)
    part_ref[...] = jnp.full(part_ref.shape, masked_sum(mask_ref, r_ref), jnp.float32)


def last_residual_kernel(pairs, all_ref, mask_ref, r_in_ref, c_hbm, r_ref, home_ref, c_ref, w_ref, terms_ref, stack_ref, sems):
    iterate_core(pairs, all_ref, mask_ref, r_in_ref, c_hbm, r_ref, c_ref, w_ref, terms_ref, stack_ref, sems)
    part = masked_sum(mask_ref, r_ref)
    n_win, count = home_ref.shape[0], home_ref.shape[1]
    rows_dev = r_ref.shape[1] * LANES // n_win
    lane = lax.broadcasted_iota(jnp.int32, (count, LANES), 1)
    for j in range(n_win):
        b, off = divmod(j * rows_dev, LANES)
        piece = r_ref[:, b, :]
        if off:
            piece = pltpu.roll(piece, LANES - off, 1)
        if off + rows_dev > LANES:
            more = pltpu.roll(r_ref[:, b + 1, :], LANES - off, 1)
            piece = jnp.where(lane < LANES - off, piece, more)
        home_ref[j] = jnp.where(lane < rows_dev, piece, part)


def spectrum_kernel(
    pairs, all_ref, mask_ref, r_in_ref, c_hbm, table_ref, o_ref, c_ref, w_ref, terms_ref, stack_ref, sems
):
    start_all(c_hbm, c_ref, sems)
    set_weights(pairs, jnp.sum(all_ref[...]) * (1.0 / LANES), mask_ref, r_in_ref, w_ref)

    def one(s, carry):
        pltpu.make_async_copy(c_hbm.at[s], c_ref.at[s], sems.at[s]).wait()
        weighted_sums(c_ref, s, w_ref.at[s], terms_ref)
        return carry

    lax.fori_loop(0, c_ref.shape[0], one, 0)
    finish_stacks(terms_ref, stack_ref)
    lane = lax.broadcasted_iota(jnp.int32, (L, LANES), 1)
    stacks = stack_ref[0]
    for s in range(1, c_ref.shape[0]):
        stacks = jnp.where(lane // 16 == s, stack_ref[s], stacks)
    both = jnp.dot(table_ref[...], stacks, precision=HIGHEST, preferred_element_type=jnp.float32)
    freq_count = table_ref.shape[0] // 2
    part = lax.broadcasted_iota(jnp.int32, (freq_count, LANES), 1) % 4
    o_ref[...] = jnp.where(part == 0, both[:freq_count], jnp.where(part == 1, both[freq_count:], 0.0))


def beam_kernel(gain, x_ref, cos_ref, sin_ref, fine_cos_ref, fine_sin_ref, o_ref):
    x = x_ref[...]
    yc = lax.dot_general(x, cos_ref[...], TN, precision=HIGHEST, preferred_element_type=jnp.float32)
    ys = lax.dot_general(x, sin_ref[...], TN, precision=HIGHEST, preferred_element_type=jnp.float32)
    c, s = fine_cos_ref[...], fine_sin_ref[...]
    u = yc * c - ys * s
    v = ys * c + yc * s
    rows = o_ref.shape[1] * 2
    out = lax.broadcasted_iota(jnp.int32, (rows, LANES), 0)
    lane = lax.broadcasted_iota(jnp.int32, (rows, LANES), 1)
    same = lane // 16 == out // 2
    imag, part = out % 2, lane % 4
    pick_u = jnp.where(same & (part == imag), 1.0, 0.0)
    pick_v = jnp.where(same & (part == 0) & (imag == 1), 1.0, 0.0) - jnp.where(
        same & (part == 1) & (imag == 0), 1.0, 0.0
    )
    beams = jnp.dot(pick_u, u, precision=HIGHEST, preferred_element_type=jnp.float32) + jnp.dot(
        pick_v, v, precision=HIGHEST, preferred_element_type=jnp.float32
    )
    for i in range(o_ref.shape[1]):
        o_ref[0, i] = beams[2 * i:2 * i + 2] * gain


def cos_sin(freq_id, chan_ids, slow_count, modulus):
    slow_ids = jnp.arange(slow_count, dtype=jnp.int32) - slow_count // 2
    phase_ids = jnp.mod((freq_id * chan_ids)[:, None] * slow_ids[None, :], modulus)
    angles = 2.0 * math.pi / modulus * phase_ids.astype(jnp.float32)
    return jnp.cos(angles), jnp.sin(angles)


VMEM = pl.BlockSpec(memory_space=pltpu.VMEM)
SMEM = pl.BlockSpec(memory_space=pltpu.SMEM)
ANY = pl.BlockSpec(memory_space=pl.ANY)


def body(spectra, sources, valid):
    win_dev, chan_dev, width = spectra.shape
    freq_count = width // 2
    source_total = sources.shape[0]
    n_win = lax.axis_size("win")
    n_ch = lax.axis_size("ch")
    n_all = n_win * n_ch
    chans = chan_dev * n_ch
    pairs = float(source_total * chans)
    win, ch = lax.axis_index("win"), lax.axis_index("ch")
    y, core = ch // 2, ch % 2
    inverse_np, forward_np = tables(freq_count, L)
    flat = spectra.reshape(win_dev * chan_dev, width)
    rows_dev = win_dev * Q
    rows = n_win * rows_dev
    piece = win_dev * width // LANES

    picked = pl.pallas_call(
        pick_kernel,
        in_specs=[SMEM, VMEM],
        out_specs=VMEM,
        out_shape=jax.ShapeDtypeStruct((source_total, piece, LANES), jnp.bfloat16),
        compiler_params=PARAMS,
        name="pick",
    )(sources, flat)
    got = lax.all_to_all(picked, "ch", 0, 0, tiled=True)
    own_mask = valid.astype(jnp.float32)
    mask_lanes = jnp.broadcast_to(own_mask.reshape(win_dev // 4, 1, 4), (win_dev // 4, Q, 4)).reshape(1, rows_dev)
    own = pl.pallas_call(
        own_kernel,
        in_specs=[VMEM, VMEM],
        out_specs=VMEM,
        out_shape=jax.ShapeDtypeStruct((n_win, piece + 8, LANES), jnp.bfloat16),
        compiler_params=PARAMS,
        name="own",
    )(got, jnp.pad(mask_lanes, ((0, 0), (0, LANES - rows_dev))))

    own = lax.all_to_all(own, "win", 0, 0, tiled=True)

    def turn_y(d):
        return [(i * 2 + c, ((i + d) % 4) * 2 + c) for i in range(n_ch // 2) for c in range(2)]

    with jax.named_scope("along_y"):
        mine = jnp.stack([own] + [lax.ppermute(own, "ch", turn_y(d)) for d in (1, 2, 3)])
    with jax.named_scope("cores"):
        theirs = lax.ppermute(mine, "ch", [(i, i ^ 1) for i in range(n_ch)])
    steps = jnp.arange(4, dtype=jnp.int32)
    slot_y = 2 * ((y - steps) % 4)
    ids = jnp.concatenate([slot_y + core, slot_y + 1 - core]).astype(jnp.int32)

    with jax.named_scope("main"):
        packed = pl.pallas_call(
            pack_kernel,
            in_specs=[VMEM],
            out_specs=VMEM,
            out_shape=jax.ShapeDtypeStruct((n_win, rows_dev, width), jnp.bfloat16),
            compiler_params=PARAMS,
            name="pack",
        )(flat)
        moved = lax.all_to_all(packed, "win", 0, 0, tiled=True)

    corr_shape = jax.ShapeDtypeStruct((source_total, L, rows), jnp.bfloat16)
    r_shape = jax.ShapeDtypeStruct((source_total, rows // LANES, LANES), jnp.float32)
    mask_shape = jax.ShapeDtypeStruct((rows // LANES, LANES), jnp.float32)
    part_shape = jax.ShapeDtypeStruct((n_all, LANES), jnp.float32)
    held = pltpu.VMEM(corr_shape.shape, jnp.bfloat16)
    row_weights = pltpu.VMEM(r_shape.shape, jnp.float32)
    terms = pltpu.VMEM((source_total, L + 16, 3 * LANES), jnp.bfloat16)
    stack = pltpu.VMEM((source_total, L, LANES), jnp.float32)
    cross = pltpu.VMEM((rows // 2, width), jnp.bfloat16)
    sems = pltpu.SemaphoreType.DMA((source_total,))
    corr, r, part, mask = pl.pallas_call(
        correlate_kernel,
        in_specs=[SMEM, VMEM, VMEM, VMEM],
        out_specs=[ANY, VMEM, VMEM, VMEM],
        out_shape=[corr_shape, r_shape, part_shape, mask_shape],
        scratch_shapes=[cross, cross, held, terms, stack, sems],
        compiler_params=pltpu.CompilerParams(vmem_limit_bytes=56 << 20),
        name="correlate",
    )(ids, moved.reshape(rows, width), jnp.concatenate([mine, theirs]), jnp.asarray(inverse_np, jnp.bfloat16))

    parts = lax.all_to_all(part, ("win", "ch"), 0, 0, tiled=True)
    for kernel, shape in (
        (iterate_kernel, part_shape),
        (last_residual_kernel, jax.ShapeDtypeStruct((n_win, source_total, LANES), jnp.float32)),
    ):
        r, part = pl.pallas_call(
            lambda *refs: kernel(pairs, *refs),
            in_specs=[VMEM, VMEM, VMEM, ANY],
            out_specs=[VMEM, VMEM],
            out_shape=[r_shape, shape],
            scratch_shapes=[held, row_weights, terms, stack, sems],
            compiler_params=BIG,
            name="iterate",
        )(parts, mask, r, corr)
        if kernel is iterate_kernel:
            parts = lax.all_to_all(part, ("win", "ch"), 0, 0, tiled=True)

    back = lax.all_to_all(part, "win", 0, 0, tiled=True)
    over_win = jnp.sum(back[:, 0, rows_dev])
    parts = lax.all_to_all(jnp.broadcast_to(over_win, (n_ch, LANES)), "ch", 0, 0, tiled=True)

    spectrum = pl.pallas_call(
        lambda *refs: spectrum_kernel(pairs, *refs),
        in_specs=[VMEM, VMEM, VMEM, ANY, VMEM],
        out_specs=VMEM,
        out_shape=jax.ShapeDtypeStruct((freq_count, LANES), jnp.float32),
        scratch_shapes=[held, row_weights, terms, stack, sems],
        compiler_params=BIG,
        name="spectrum",
    )(parts, mask, r, corr, jnp.asarray(forward_np))
    pieces = lax.all_to_all(spectrum, ("win", "ch"), 0, 0, tiled=True)

    freq_id = win * n_ch + ch
    modulus = 4 * freq_count * P_SIZE
    device = jnp.arange(n_all, dtype=jnp.int32)
    coarse = (device % n_ch) * chan_dev + (device // n_ch) * Q
    cosines, sines = cos_sin(freq_id, coarse, P_SIZE, modulus)
    fine_cos, fine_sin = cos_sin(freq_id, (jnp.arange(LANES, dtype=jnp.int32) // 4) % Q, P_SIZE, modulus)
    beamed = pl.pallas_call(
        lambda *refs: beam_kernel(chans ** (-0.5), *refs),
        in_specs=[VMEM] * 5,
        out_specs=VMEM,
        out_shape=jax.ShapeDtypeStruct((1, source_total, 2, P_SIZE), jnp.float32),
        compiler_params=PARAMS,
        name="beam",
    )(pieces, cosines, sines, fine_cos, fine_sin)

    window_count = jnp.sum(mask) * (1.0 / Q)
    spread_sq = jnp.sum(parts[:, 0]) / (pairs * window_count) + epsilon
    residual = back[:, :, :rows_dev].reshape(n_win, source_total, win_dev // 4, Q, 4)
    residual = residual.transpose(2, 4, 1, 0, 3).reshape(win_dev, source_total, chan_dev)
    weights = own_mask[:, None, None] * (degrees + 1.0) / (degrees + residual / spread_sq)
    return (weights, beamed)


def solution(mesh):
    return jax.shard_map(
        body,
        mesh=mesh,
        in_specs=(P("win", "ch", None), P(), P("win")),
        out_specs=(P("win", None, "ch"), P(("win", "ch"), None, None, None)),
        check_vma=False,
    )
```

```python
import math

import jax
import jax.numpy as jnp
import numpy as np
from jax import lax
from jax.experimental import pallas as pl
from jax.experimental.pallas import tpu as pltpu
from jax.sharding import PartitionSpec as P

L = 256
P_SIZE = 512
ITERS = 3
Q = 4
LANES = 128
PARAMS = pltpu.CompilerParams(vmem_limit_bytes=16 << 20)

degrees = 3.0
epsilon = 1e-06
HIGHEST = lax.Precision.HIGHEST
NT = (((1,), (1,)), ((), ()))
TN = (((0,), (0,)), ((), ()))


def tables(freq_count, lag_count):
    freq_ids = np.arange(freq_count, dtype=np.int64)
    delays = np.arange(lag_count, dtype=np.int64) - lag_count // 2
    phase_ids = np.mod(freq_ids[:, None] * delays[None, :], 2 * freq_count)
    angles = np.float32(2.0 * math.pi / (2 * freq_count)) * phase_ids.astype(np.float32)
    cosines = np.cos(angles.astype(np.float64)).astype(np.float32)
    sines = np.sin(angles.astype(np.float64)).astype(np.float32)
    inverse_factor = np.float32(1.0 / math.sqrt(freq_count))
    forward_factor = np.float32(1.0 / math.sqrt(lag_count))
    inverse = np.concatenate([cosines * inverse_factor, -sines * inverse_factor], axis=0)
    forward = np.concatenate([cosines * forward_factor, -sines * forward_factor], axis=0)
    return np.ascontiguousarray(inverse.T), forward


def pick_kernel(sources_ref, x_ref, o_ref):
    rows, count = x_ref.shape[0], o_ref.shape[0]
    chan_dev = 128
    row = lax.broadcasted_iota(jnp.int32, (24, rows), 0)
    col = lax.broadcasted_iota(jnp.int32, (24, rows), 1)
    window = (row // 8) * 4 + row % 4
    shift = lax.axis_index("ch") * chan_dev
    blocks = []
    for s in range(count):
        base = sources_ref[s] - shift
        base = jnp.where((base >= 0) & (base < chan_dev), base, -(1 << 20))
        blocks.append(jnp.where(col == window * chan_dev + base, 1.0, 0.0))
    picker = jnp.concatenate(blocks, axis=0).astype(jnp.bfloat16)
    picked = jnp.dot(picker, x_ref[...], preferred_element_type=jnp.float32).reshape(count, 24, 512)
    low = lax.broadcasted_iota(jnp.int32, (8, LANES), 0) < 4
    for s in range(count):
        for t in range(3):
            tile = picked[s, t * 8:(t + 1) * 8, :]
            pair = [
                jnp.where(low, tile[:, p * 256:p * 256 + 128], tile[:, p * 256 + 128:p * 256 + 256])
                for p in range(2)
            ]
            o_ref[s, t * 16:(t + 1) * 16, :] = jnp.concatenate(pair, axis=0).astype(jnp.bfloat16)


def own_kernel(x_ref, mask_ref, o_ref):
    total = x_ref[0].astype(jnp.float32)
    for g in range(1, x_ref.shape[0]):
        total += x_ref[g].astype(jnp.float32)
    rows = total.shape[0]
    masks = jnp.broadcast_to(mask_ref[...], (8, LANES))
    block = jnp.concatenate([total, masks], axis=0).astype(jnp.bfloat16)
    for j in range(o_ref.shape[0]):
        o_ref[j] = block


def pack_kernel(x_ref, o_ref):
    row = lax.broadcasted_iota(jnp.int32, (512, 512), 0)
    col = lax.broadcasted_iota(jnp.int32, (512, 512), 1)
    src = (row % 4) * 128 + (row // 16) * 4 + (row // 4) % 4
    perm = jnp.where(col == src, 1.0, 0.0).astype(jnp.bfloat16)
    for t in range(o_ref.shape[1] // 16):
        got = jnp.dot(perm, x_ref[t * 512:(t + 1) * 512, :], preferred_element_type=jnp.float32)
        o_ref[:, t * 16:(t + 1) * 16, :] = got.astype(jnp.bfloat16).reshape(
            o_ref.shape[0], 16, x_ref.shape[1]
        )


LAG_CHUNK = 64


def three_terms(x):
    high = x.astype(jnp.bfloat16)
    rest = x - high.astype(jnp.float32)
    middle = rest.astype(jnp.bfloat16)
    low = (rest - middle.astype(jnp.float32)).astype(jnp.bfloat16)
    return high, middle, low


def same_channel():
    a = lax.broadcasted_iota(jnp.int32, (3 * LANES, LANES), 0)
    b = lax.broadcasted_iota(jnp.int32, (3 * LANES, LANES), 1)
    return jnp.where((a // 4) % 4 == (b // 4) % 4, 1.0, 0.0).astype(jnp.bfloat16)


def weighted_sums(c_ref, s, w_rows, terms_ref):
    weights = [w_rows[b:b + 1, :] for b in range(w_rows.shape[0])]
    for k in range(L // LAG_CHUNK):
        lags = slice(k * LAG_CHUNK, (k + 1) * LAG_CHUNK)
        acc = jnp.zeros((LAG_CHUNK, LANES), jnp.float32)
        for b, w in enumerate(weights):
            acc += w * c_ref[s, lags, b * LANES:(b + 1) * LANES].astype(jnp.float32)
        for i, term in enumerate(three_terms(acc)):
            terms_ref[s, lags, i * LANES:(i + 1) * LANES] = term
    weight_sum = jnp.broadcast_to(jnp.sum(w_rows[...], axis=0, keepdims=True), (16, LANES))
    for i, term in enumerate(three_terms(weight_sum)):
        terms_ref[s, L:L + 16, i * LANES:(i + 1) * LANES] = term


def finish_stacks(terms_ref, stack_ref):
    group = same_channel()
    for s in range(terms_ref.shape[0]):
        sums = jnp.dot(terms_ref[s], group, preferred_element_type=jnp.float32)
        stack_ref[s] = sums[:L] * (1.0 / sums[L:L + 1])


def residuals(c_ref, s, stack_ref, r_ref):
    for b in range(r_ref.shape[1]):
        total = jnp.zeros((8, LANES), jnp.float32)
        for k in range(L // LAG_CHUNK):
            lags = slice(k * LAG_CHUNK, (k + 1) * LAG_CHUNK)
            d = c_ref[s, lags, b * LANES:(b + 1) * LANES].astype(jnp.float32) - stack_ref[s, lags, :]
            total += jnp.sum((d * d).reshape(LAG_CHUNK // 8, 8, LANES), axis=0)
        r_ref[s, b:b + 1, :] = jnp.sum(total, axis=0, keepdims=True) * (1.0 / L)


def masked_sum(mask_ref, r_ref):
    return jnp.sum(mask_ref[...][None] * r_ref[...])


def correlate_kernel(
    ids_ref, a_ref, x_ref, y_ref, inv_ref, c_ref, r_ref, part_ref, mask_ref, even_ref, odd_ref, terms_ref, stack_ref
):
    n_win, rows = x_ref.shape[1], a_ref.shape[0]
    half = a_ref.shape[1] // 2
    rows_dev = rows // n_win
    low = lax.broadcasted_iota(jnp.int32, (8, LANES), 0) < 4

    lane = lax.broadcasted_iota(jnp.int32, (8, LANES), 1)
    pieces = [jnp.zeros((8, LANES), jnp.float32) for _ in range(rows // LANES)]
    for j in range(n_win):
        row = x_ref[0, j, 48:56, :].astype(jnp.float32)
        b, off = divmod(j * rows_dev, LANES)
        turned = pltpu.roll(row, off, 1) if off else row
        end = off + rows_dev
        pieces[b] = jnp.where((lane >= off) & (lane < end), turned, pieces[b])
        if end > LANES:
            pieces[b + 1] = jnp.where(lane < end - LANES, turned, pieces[b + 1])
    for b, piece in enumerate(pieces):
        mask_ref[b:b + 1, :] = piece[0:1, :]

    count, half_rows = c_ref.shape[0], rows // 2
    half_win = n_win // 2

    def fill(cross_ref, s_ref, k, side):
        for j in range(half_win):
            for t in range(3):
                quarters = []
                for p in range(2):
                    at = t * 16 + p * 8
                    tile = s_ref[k, side * half_win + j, at:at + 8, :].astype(jnp.float32)
                    turned = pltpu.roll(tile, 4, 0)
                    quarters += [jnp.where(low, tile, turned), jnp.where(low, turned, tile)]
                at = slice(j * rows_dev + t * 16, j * rows_dev + t * 16 + 16)
                src = slice(at.start + side * half_rows, at.stop + side * half_rows)
                for i in range(2):
                    a = jnp.concatenate([quarters[i]] * 2, axis=0)
                    b = jnp.concatenate([quarters[2 + i]] * 2, axis=0)
                    first = slice(i * LANES, (i + 1) * LANES)
                    second = slice(half + i * LANES, half + (i + 1) * LANES)
                    u = a_ref[src, first].astype(jnp.float32)
                    v = a_ref[src, second].astype(jnp.float32)
                    cross_ref[at, first] = (a * u + b * v).astype(jnp.bfloat16)
                    cross_ref[at, second] = (b * u - a * v).astype(jnp.bfloat16)

    def correlate(cross_ref, s, side):
        for n in range(half_rows // 256):
            got = lax.dot_general(
                inv_ref[...], cross_ref[n * 256:(n + 1) * 256, :], NT, preferred_element_type=jnp.float32
            )
            at = side * half_rows + n * 256
            c_ref[s, :, at:at + 256] = got.astype(jnp.bfloat16)

    fill(even_ref, x_ref, 0, 0)
    pairs_of_slots = count // 2

    def slot(k, carry):
        after = jnp.minimum(k + 1, pairs_of_slots - 1)
        for s, s_ref, next_ref, next_k in (
            (ids_ref[k], x_ref, y_ref, k),
            (ids_ref[pairs_of_slots + k], y_ref, x_ref, after),
        ):
            correlate(even_ref, s, 0)
            fill(odd_ref, s_ref, k, 1)
            correlate(odd_ref, s, 1)
            fill(even_ref, next_ref, next_k, 0)
            weighted_sums(c_ref, s, mask_ref, terms_ref)
        return carry

    lax.fori_loop(0, pairs_of_slots, slot, 0)
    finish_stacks(terms_ref, stack_ref)

    def last(s, carry):
        residuals(c_ref, s, stack_ref, r_ref)
        return carry

    lax.fori_loop(0, count, last, 0)
    part_ref[...] = jnp.full(part_ref.shape, masked_sum(mask_ref, r_ref), jnp.float32)


def set_weights(pairs, total, mask_ref, r_ref, w_ref):
    mask = mask_ref[...]
    spread = total / (pairs * jnp.sum(mask) * (1.0 / Q)) + epsilon
    w_ref[...] = mask[None] * (degrees + 1.0) / (degrees + r_ref[...] / spread)
    return spread


def iterate_core(pairs, all_ref, mask_ref, r_in_ref, c_ref, r_ref, w_ref, terms_ref, stack_ref):
    set_weights(pairs, jnp.sum(all_ref[...]) * (1.0 / LANES), mask_ref, r_in_ref, w_ref)

    def one(s, carry):
        weighted_sums(c_ref, s, w_ref.at[s], terms_ref)
        return carry

    lax.fori_loop(0, c_ref.shape[0], one, 0)
    finish_stacks(terms_ref, stack_ref)

    def last(s, carry):
        residuals(c_ref, s, stack_ref, r_ref)
        return carry

    lax.fori_loop(0, c_ref.shape[0], last, 0)


def iterate_kernel(pairs, all_ref, mask_ref, r_in_ref, c_ref, r_ref, part_ref, w_ref, terms_ref, stack_ref):
    iterate_core(pairs, all_ref, mask_ref, r_in_ref, c_ref, r_ref, w_ref, terms_ref, stack_ref)
    part_ref[...] = jnp.full(part_ref.shape, masked_sum(mask_ref, r_ref), jnp.float32)


def last_residual_kernel(pairs, all_ref, mask_ref, r_in_ref, c_ref, r_ref, home_ref, w_ref, terms_ref, stack_ref):
    iterate_core(pairs, all_ref, mask_ref, r_in_ref, c_ref, r_ref, w_ref, terms_ref, stack_ref)
    part = masked_sum(mask_ref, r_ref)
    n_win, count = home_ref.shape[0], home_ref.shape[1]
    rows_dev = r_ref.shape[1] * LANES // n_win
    lane = lax.broadcasted_iota(jnp.int32, (count, LANES), 1)
    for j in range(n_win):
        b, off = divmod(j * rows_dev, LANES)
        piece = r_ref[:, b, :]
        if off:
            piece = pltpu.roll(piece, LANES - off, 1)
        if off + rows_dev > LANES:
            more = pltpu.roll(r_ref[:, b + 1, :], LANES - off, 1)
            piece = jnp.where(lane < LANES - off, piece, more)
        home_ref[j] = jnp.where(lane < rows_dev, piece, part)


def carry_kernel(lane_id, x_ref, o_ref):
    total = jnp.sum(x_ref[...], axis=0)
    lane = lax.broadcasted_iota(jnp.int32, total.shape, 1)
    row = lax.broadcasted_iota(jnp.int32, total.shape, 0)
    o_ref[...] = jnp.full(o_ref.shape, jnp.sum(jnp.where((lane == lane_id) & (row == 0), total, 0.0)), jnp.float32)


def spectrum_kernel(
    pairs, all_ref, mask_ref, r_in_ref, c_ref, table_ref, o_ref, spread_ref, w_ref, terms_ref, stack_ref
):
    spread = set_weights(pairs, jnp.sum(all_ref[...]) * (1.0 / LANES), mask_ref, r_in_ref, w_ref)

    def one(s, carry):
        weighted_sums(c_ref, s, w_ref.at[s], terms_ref)
        return carry

    lax.fori_loop(0, c_ref.shape[0], one, 0)
    finish_stacks(terms_ref, stack_ref)
    spread_ref[...] = jnp.full(spread_ref.shape, spread, jnp.float32)
    lane = lax.broadcasted_iota(jnp.int32, (L, LANES), 1)
    stacks = stack_ref[0]
    for s in range(1, c_ref.shape[0]):
        stacks = jnp.where(lane // 16 == s, stack_ref[s], stacks)
    both = jnp.dot(table_ref[...], stacks, precision=HIGHEST, preferred_element_type=jnp.float32)
    freq_count = table_ref.shape[0] // 2
    part = lax.broadcasted_iota(jnp.int32, (freq_count, LANES), 1) % 4
    o_ref[...] = jnp.where(part == 0, both[:freq_count], jnp.where(part == 1, both[freq_count:], 0.0))


def beam_kernel(gain, x_ref, cos_ref, sin_ref, fine_cos_ref, fine_sin_ref, o_ref):
    x = x_ref[...]
    yc = lax.dot_general(x, cos_ref[...], TN, precision=HIGHEST, preferred_element_type=jnp.float32)
    ys = lax.dot_general(x, sin_ref[...], TN, precision=HIGHEST, preferred_element_type=jnp.float32)
    c, s = fine_cos_ref[...], fine_sin_ref[...]
    u = yc * c - ys * s
    v = ys * c + yc * s
    rows = o_ref.shape[1] * 2
    out = lax.broadcasted_iota(jnp.int32, (rows, LANES), 0)
    lane = lax.broadcasted_iota(jnp.int32, (rows, LANES), 1)
    same = lane // 16 == out // 2
    imag, part = out % 2, lane % 4
    pick_u = jnp.where(same & (part == imag), 1.0, 0.0)
    pick_v = jnp.where(same & (part == 0) & (imag == 1), 1.0, 0.0) - jnp.where(
        same & (part == 1) & (imag == 0), 1.0, 0.0
    )
    beams = jnp.dot(pick_u, u, precision=HIGHEST, preferred_element_type=jnp.float32) + jnp.dot(
        pick_v, v, precision=HIGHEST, preferred_element_type=jnp.float32
    )
    for i in range(o_ref.shape[1]):
        o_ref[0, i] = beams[2 * i:2 * i + 2] * gain


def cos_sin(freq_id, chan_ids, slow_count, modulus):
    slow_ids = jnp.arange(slow_count, dtype=jnp.int32) - slow_count // 2
    phase_ids = jnp.mod((freq_id * chan_ids)[:, None] * slow_ids[None, :], modulus)
    angles = 2.0 * math.pi / modulus * phase_ids.astype(jnp.float32)
    return jnp.cos(angles), jnp.sin(angles)


VMEM = pl.BlockSpec(memory_space=pltpu.VMEM)
SMEM = pl.BlockSpec(memory_space=pltpu.SMEM)


def body(spectra, sources, valid):
    win_dev, chan_dev, width = spectra.shape
    freq_count = width // 2
    source_total = sources.shape[0]
    n_win = lax.axis_size("win")
    n_ch = lax.axis_size("ch")
    n_all = n_win * n_ch
    chans = chan_dev * n_ch
    pairs = float(source_total * chans)
    win, ch = lax.axis_index("win"), lax.axis_index("ch")
    y, core = ch // 2, ch % 2
    inverse_np, forward_np = tables(freq_count, L)
    flat = spectra.reshape(win_dev * chan_dev, width)
    rows_dev = win_dev * Q
    rows = n_win * rows_dev
    piece = win_dev * width // LANES

    picked = pl.pallas_call(
        pick_kernel,
        in_specs=[SMEM, VMEM],
        out_specs=VMEM,
        out_shape=jax.ShapeDtypeStruct((source_total, piece, LANES), jnp.bfloat16),
        compiler_params=PARAMS,
        name="pick",
    )(sources, flat)
    got = lax.all_to_all(picked, "ch", 0, 0, tiled=True)
    own_mask = valid.astype(jnp.float32)
    mask_lanes = jnp.broadcast_to(own_mask.reshape(win_dev // 4, 1, 4), (win_dev // 4, Q, 4)).reshape(1, rows_dev)
    own = pl.pallas_call(
        own_kernel,
        in_specs=[VMEM, VMEM],
        out_specs=VMEM,
        out_shape=jax.ShapeDtypeStruct((n_win, piece + 8, LANES), jnp.bfloat16),
        compiler_params=PARAMS,
        name="own",
    )(got, jnp.pad(mask_lanes, ((0, 0), (0, LANES - rows_dev))))

    own = lax.all_to_all(own, "win", 0, 0, tiled=True)

    def turn_y(d):
        return [(i * 2 + c, ((i + d) % 4) * 2 + c) for i in range(n_ch // 2) for c in range(2)]

    with jax.named_scope("along_y"):
        mine = jnp.stack([own] + [lax.ppermute(own, "ch", turn_y(d)) for d in (1, 2, 3)])
    with jax.named_scope("cores"):
        theirs = lax.ppermute(mine, "ch", [(i, i ^ 1) for i in range(n_ch)])
    steps = jnp.arange(4, dtype=jnp.int32)
    slot_y = 2 * ((y - steps) % 4)
    ids = jnp.concatenate([slot_y + core, slot_y + 1 - core]).astype(jnp.int32)

    with jax.named_scope("main"):
        packed = pl.pallas_call(
            pack_kernel,
            in_specs=[VMEM],
            out_specs=VMEM,
            out_shape=jax.ShapeDtypeStruct((n_win, rows_dev, width), jnp.bfloat16),
            compiler_params=PARAMS,
            name="pack",
        )(flat)
        moved = lax.all_to_all(packed, "win", 0, 0, tiled=True)

    freq_id = win * n_ch + ch
    modulus = 4 * freq_count * P_SIZE
    device = jnp.arange(n_all, dtype=jnp.int32)
    coarse = (device % n_ch) * chan_dev + (device // n_ch) * Q
    cosines, sines = cos_sin(freq_id, coarse, P_SIZE, modulus)
    fine_cos, fine_sin = cos_sin(freq_id, (jnp.arange(LANES, dtype=jnp.int32) // 4) % Q, P_SIZE, modulus)
    moved, cosines, sines, fine_cos, fine_sin = lax.optimization_barrier(
        (moved, cosines, sines, fine_cos, fine_sin)
    )

    corr_shape = jax.ShapeDtypeStruct((source_total, L, rows), jnp.bfloat16)
    r_shape = jax.ShapeDtypeStruct((source_total, rows // LANES, LANES), jnp.float32)
    mask_shape = jax.ShapeDtypeStruct((rows // LANES, LANES), jnp.float32)
    part_shape = jax.ShapeDtypeStruct((n_all, LANES), jnp.float32)
    row_weights = pltpu.VMEM(r_shape.shape, jnp.float32)
    terms = pltpu.VMEM((source_total, L + 16, 3 * LANES), jnp.bfloat16)
    stack = pltpu.VMEM((source_total, L, LANES), jnp.float32)
    cross = pltpu.VMEM((rows // 2, width), jnp.bfloat16)
    corr, r, part, mask = pl.pallas_call(
        correlate_kernel,
        in_specs=[SMEM] + [VMEM] * 4,
        out_specs=[VMEM] * 4,
        out_shape=[corr_shape, r_shape, part_shape, mask_shape],
        scratch_shapes=[cross, cross, terms, stack],
        compiler_params=PARAMS,
        name="correlate",
    )(ids, moved.reshape(rows, width), mine, theirs, jnp.asarray(inverse_np, jnp.bfloat16))

    parts = lax.all_to_all(part, ("win", "ch"), 0, 0, tiled=True)
    for kernel, shape in (
        (iterate_kernel, part_shape),
        (last_residual_kernel, jax.ShapeDtypeStruct((n_win, source_total, LANES), jnp.float32)),
    ):
        r, part = pl.pallas_call(
            lambda *refs: kernel(pairs, *refs),
            in_specs=[VMEM] * 4,
            out_specs=[VMEM, VMEM],
            out_shape=[r_shape, shape],
            scratch_shapes=[row_weights, terms, stack],
            compiler_params=PARAMS,
            name="iterate",
        )(parts, mask, r, corr)
        if kernel is iterate_kernel:
            parts = lax.all_to_all(part, ("win", "ch"), 0, 0, tiled=True)

    back = lax.all_to_all(part, "win", 0, 0, tiled=True)
    over_win = pl.pallas_call(
        lambda *refs: carry_kernel(rows_dev, *refs),
        in_specs=[VMEM],
        out_specs=VMEM,
        out_shape=jax.ShapeDtypeStruct((n_ch, LANES), jnp.float32),
        compiler_params=PARAMS,
        name="carry",
    )(back)
    parts = lax.all_to_all(over_win, "ch", 0, 0, tiled=True)

    spectrum, spread_sq = pl.pallas_call(
        lambda *refs: spectrum_kernel(pairs, *refs),
        in_specs=[VMEM] * 5,
        out_specs=[VMEM] * 2,
        out_shape=[
            jax.ShapeDtypeStruct((freq_count, LANES), jnp.float32),
            jax.ShapeDtypeStruct((8, LANES), jnp.float32),
        ],
        scratch_shapes=[row_weights, terms, stack],
        compiler_params=PARAMS,
        name="spectrum",
    )(parts, mask, r, corr, jnp.asarray(forward_np))
    pieces = lax.all_to_all(spectrum, ("win", "ch"), 0, 0, tiled=True)

    beamed = pl.pallas_call(
        lambda *refs: beam_kernel(chans ** (-0.5), *refs),
        in_specs=[VMEM] * 5,
        out_specs=VMEM,
        out_shape=jax.ShapeDtypeStruct((1, source_total, 2, P_SIZE), jnp.float32),
        compiler_params=PARAMS,
        name="beam",
    )(pieces, cosines, sines, fine_cos, fine_sin)

    own_mask, back, spread_sq = lax.optimization_barrier((own_mask, back, spread_sq[0, 0]))
    residual = back[:, :, :rows_dev].reshape(n_win, source_total, win_dev // 4, Q, 4)
    residual = residual.transpose(2, 4, 1, 0, 3).reshape(win_dev, source_total, chan_dev)
    weights = own_mask[:, None, None] * (degrees + 1.0) / (degrees + residual / spread_sq)
    return (weights, beamed)


def solution(mesh):
    return jax.shard_map(
        body,
        mesh=mesh,
        in_specs=(P("win", "ch", None), P(), P("win")),
        out_specs=(P("win", None, "ch"), P(("win", "ch"), None, None, None)),
        check_vma=False,
    )
```

```python
import math

import jax
import jax.numpy as jnp
import numpy as np
from jax import lax
from jax.experimental import pallas as pl
from jax.experimental.pallas import tpu as pltpu
from jax.sharding import PartitionSpec as P

L = 256
P_SIZE = 512
ITERS = 3
Q = 4
LANES = 128
PARAMS = pltpu.CompilerParams(vmem_limit_bytes=16 << 20)

degrees = 3.0
epsilon = 1e-06
HIGHEST = lax.Precision.HIGHEST
NT = (((1,), (1,)), ((), ()))
TN = (((0,), (0,)), ((), ()))


def tables(freq_count, lag_count):
    freq_ids = np.arange(freq_count, dtype=np.int64)
    delays = np.arange(lag_count, dtype=np.int64) - lag_count // 2
    phase_ids = np.mod(freq_ids[:, None] * delays[None, :], 2 * freq_count)
    angles = np.float32(2.0 * math.pi / (2 * freq_count)) * phase_ids.astype(np.float32)
    cosines = np.cos(angles.astype(np.float64)).astype(np.float32)
    sines = np.sin(angles.astype(np.float64)).astype(np.float32)
    inverse_factor = np.float32(1.0 / math.sqrt(freq_count))
    forward_factor = np.float32(1.0 / math.sqrt(lag_count))
    inverse = np.concatenate([cosines * inverse_factor, -sines * inverse_factor], axis=0)
    forward = np.concatenate([cosines * forward_factor, -sines * forward_factor], axis=0)
    return np.ascontiguousarray(inverse.T), forward


def pick_kernel(sources_ref, x_ref, o_ref):
    rows, count = x_ref.shape[0], o_ref.shape[0]
    chan_dev = 128
    row = lax.broadcasted_iota(jnp.int32, (24, rows), 0)
    col = lax.broadcasted_iota(jnp.int32, (24, rows), 1)
    window = (row // 8) * 4 + row % 4
    shift = lax.axis_index("ch") * chan_dev
    blocks = []
    for s in range(count):
        base = sources_ref[s] - shift
        base = jnp.where((base >= 0) & (base < chan_dev), base, -(1 << 20))
        blocks.append(jnp.where(col == window * chan_dev + base, 1.0, 0.0))
    picker = jnp.concatenate(blocks, axis=0).astype(jnp.bfloat16)
    picked = jnp.dot(picker, x_ref[...], preferred_element_type=jnp.float32).reshape(count, 24, 512)
    low = lax.broadcasted_iota(jnp.int32, (8, LANES), 0) < 4
    for s in range(count):
        for t in range(3):
            tile = picked[s, t * 8:(t + 1) * 8, :]
            pair = [
                jnp.where(low, tile[:, p * 256:p * 256 + 128], tile[:, p * 256 + 128:p * 256 + 256])
                for p in range(2)
            ]
            o_ref[s, t * 16:(t + 1) * 16, :] = jnp.concatenate(pair, axis=0).astype(jnp.bfloat16)


def own_kernel(x_ref, mask_ref, o_ref):
    total = x_ref[0].astype(jnp.float32)
    for g in range(1, x_ref.shape[0]):
        total += x_ref[g].astype(jnp.float32)
    rows = total.shape[0]
    masks = jnp.broadcast_to(mask_ref[...], (8, LANES))
    block = jnp.concatenate([total, masks], axis=0).astype(jnp.bfloat16)
    for j in range(o_ref.shape[0]):
        o_ref[j] = block


def pack_kernel(x_ref, o_ref):
    row = lax.broadcasted_iota(jnp.int32, (512, 512), 0)
    col = lax.broadcasted_iota(jnp.int32, (512, 512), 1)
    src = (row % 4) * 128 + (row // 16) * 4 + (row // 4) % 4
    perm = jnp.where(col == src, 1.0, 0.0).astype(jnp.bfloat16)
    for t in range(o_ref.shape[1] // 16):
        got = jnp.dot(perm, x_ref[t * 512:(t + 1) * 512, :], preferred_element_type=jnp.float32)
        o_ref[:, t * 16:(t + 1) * 16, :] = got.astype(jnp.bfloat16).reshape(
            o_ref.shape[0], 16, x_ref.shape[1]
        )


LAG_CHUNK = 64


def three_terms(x):
    high = x.astype(jnp.bfloat16)
    rest = x - high.astype(jnp.float32)
    middle = rest.astype(jnp.bfloat16)
    low = (rest - middle.astype(jnp.float32)).astype(jnp.bfloat16)
    return high, middle, low


def same_channel():
    a = lax.broadcasted_iota(jnp.int32, (3 * LANES, LANES), 0)
    b = lax.broadcasted_iota(jnp.int32, (3 * LANES, LANES), 1)
    return jnp.where((a // 4) % 4 == (b // 4) % 4, 1.0, 0.0).astype(jnp.bfloat16)


def weighted_sums(c_ref, s, w_rows, terms_ref):
    weights = [w_rows[b:b + 1, :] for b in range(w_rows.shape[0])]
    for k in range(L // LAG_CHUNK):
        lags = slice(k * LAG_CHUNK, (k + 1) * LAG_CHUNK)
        acc = jnp.zeros((LAG_CHUNK, LANES), jnp.float32)
        for b, w in enumerate(weights):
            acc += w * c_ref[s, lags, b * LANES:(b + 1) * LANES].astype(jnp.float32)
        for i, term in enumerate(three_terms(acc)):
            terms_ref[s, lags, i * LANES:(i + 1) * LANES] = term
    weight_sum = jnp.broadcast_to(jnp.sum(w_rows[...], axis=0, keepdims=True), (16, LANES))
    for i, term in enumerate(three_terms(weight_sum)):
        terms_ref[s, L:L + 16, i * LANES:(i + 1) * LANES] = term


def finish_stack(terms_ref, s, stack_ref):
    sums = jnp.dot(terms_ref[s], same_channel(), preferred_element_type=jnp.float32)
    stack_ref[s] = sums[:L] * (1.0 / sums[L:L + 1])


def all_stacks(c_ref, w_ref, terms_ref, stack_ref):
    count = c_ref.shape[0]
    for s in range(count):
        weighted_sums(c_ref, s, w_ref.at[s], terms_ref)
        if s:
            finish_stack(terms_ref, s - 1, stack_ref)
    finish_stack(terms_ref, count - 1, stack_ref)


def residuals(c_ref, s, stack_ref, r_ref):
    for b in range(r_ref.shape[1]):
        total = jnp.zeros((8, LANES), jnp.float32)
        for k in range(L // LAG_CHUNK):
            lags = slice(k * LAG_CHUNK, (k + 1) * LAG_CHUNK)
            d = c_ref[s, lags, b * LANES:(b + 1) * LANES].astype(jnp.float32) - stack_ref[s, lags, :]
            total += jnp.sum((d * d).reshape(LAG_CHUNK // 8, 8, LANES), axis=0)
        r_ref[s, b:b + 1, :] = jnp.sum(total, axis=0, keepdims=True) * (1.0 / L)


def masked_sum(mask_ref, r_ref):
    return jnp.sum(mask_ref[...][None] * r_ref[...])


def correlate_kernel(
    ids_ref, a_ref, x_ref, y_ref, masks_ref, inv_hbm, c_ref, r_ref, part_ref, mask_ref, even_ref, odd_ref, terms_ref, stack_ref, inv_ref, sem
):
    table = pltpu.make_async_copy(inv_hbm, inv_ref, sem)
    table.start()
    n_win, rows = x_ref.shape[1], a_ref.shape[0]
    half = a_ref.shape[1] // 2
    rows_dev = rows // n_win
    z_size, x_size = 8, n_win // 8
    far = [(ids_ref[8] - x + x_size) % x_size * z_size for x in range(x_size)]
    low = lax.broadcasted_iota(jnp.int32, (8, LANES), 0) < 4

    lane = lax.broadcasted_iota(jnp.int32, (8, LANES), 1)
    pieces = [jnp.zeros((8, LANES), jnp.float32) for _ in range(rows // LANES)]
    for j in range(n_win):
        row = masks_ref[far[j // z_size] + j % z_size].astype(jnp.float32)
        b, off = divmod(j * rows_dev, LANES)
        turned = pltpu.roll(row, off, 1) if off else row
        end = off + rows_dev
        pieces[b] = jnp.where((lane >= off) & (lane < end), turned, pieces[b])
        if end > LANES:
            pieces[b + 1] = jnp.where(lane < end - LANES, turned, pieces[b + 1])
    for b, piece in enumerate(pieces):
        mask_ref[b:b + 1, :] = piece[0:1, :]

    count, half_rows = c_ref.shape[0], rows // 2
    half_win = n_win // 2

    def fill(cross_ref, s_ref, k, side):
        for j in range(half_win):
            held = far[(side * half_win + j) // z_size] + j % z_size
            for t in range(3):
                quarters = []
                for p in range(2):
                    at = t * 16 + p * 8
                    tile = s_ref[k, held, at:at + 8, :].astype(jnp.float32)
                    turned = pltpu.roll(tile, 4, 0)
                    quarters += [jnp.where(low, tile, turned), jnp.where(low, turned, tile)]
                at = slice(j * rows_dev + t * 16, j * rows_dev + t * 16 + 16)
                src = slice(at.start + side * half_rows, at.stop + side * half_rows)
                for i in range(2):
                    a = jnp.concatenate([quarters[i]] * 2, axis=0)
                    b = jnp.concatenate([quarters[2 + i]] * 2, axis=0)
                    first = slice(i * LANES, (i + 1) * LANES)
                    second = slice(half + i * LANES, half + (i + 1) * LANES)
                    u = a_ref[src, first].astype(jnp.float32)
                    v = a_ref[src, second].astype(jnp.float32)
                    cross_ref[at, first] = (a * u + b * v).astype(jnp.bfloat16)
                    cross_ref[at, second] = (b * u - a * v).astype(jnp.bfloat16)

    def correlate(cross_ref, s, side):
        for n in range(half_rows // 256):
            got = lax.dot_general(
                inv_ref[...], cross_ref[n * 256:(n + 1) * 256, :], NT, preferred_element_type=jnp.float32
            )
            at = side * half_rows + n * 256
            c_ref[s, :, at:at + 256] = got.astype(jnp.bfloat16)

    fill(even_ref, x_ref, 0, 0)
    table.wait()
    pairs_of_slots = count // 2

    def slot(k, carry):
        after = jnp.minimum(k + 1, pairs_of_slots - 1)
        for s, s_ref, next_ref, next_k in (
            (ids_ref[k], x_ref, y_ref, k),
            (ids_ref[pairs_of_slots + k], y_ref, x_ref, after),
        ):
            correlate(even_ref, s, 0)
            fill(odd_ref, s_ref, k, 1)
            correlate(odd_ref, s, 1)
            fill(even_ref, next_ref, next_k, 0)
            weighted_sums(c_ref, s, mask_ref, terms_ref)
            finish_stack(terms_ref, s, stack_ref)
        return carry

    lax.fori_loop(0, pairs_of_slots, slot, 0)

    def last(s, carry):
        residuals(c_ref, s, stack_ref, r_ref)
        return carry

    lax.fori_loop(0, count, last, 0)
    part_ref[...] = jnp.full(part_ref.shape, masked_sum(mask_ref, r_ref), jnp.float32)


def set_weights(pairs, total, mask_ref, r_ref, w_ref):
    mask = mask_ref[...]
    spread = total / (pairs * jnp.sum(mask) * (1.0 / Q)) + epsilon
    w_ref[...] = mask[None] * (degrees + 1.0) / (degrees + r_ref[...] / spread)
    return spread


def iterate_core(pairs, all_ref, mask_ref, r_in_ref, c_ref, r_ref, w_ref, terms_ref, stack_ref):
    set_weights(pairs, jnp.sum(all_ref[...]) * (1.0 / LANES), mask_ref, r_in_ref, w_ref)

    all_stacks(c_ref, w_ref, terms_ref, stack_ref)

    def last(s, carry):
        residuals(c_ref, s, stack_ref, r_ref)
        return carry

    lax.fori_loop(0, c_ref.shape[0], last, 0)


def iterate_kernel(pairs, all_ref, mask_ref, r_in_ref, c_ref, r_ref, part_ref, w_ref, terms_ref, stack_ref):
    iterate_core(pairs, all_ref, mask_ref, r_in_ref, c_ref, r_ref, w_ref, terms_ref, stack_ref)
    part_ref[...] = jnp.full(part_ref.shape, masked_sum(mask_ref, r_ref), jnp.float32)


def last_residual_kernel(pairs, all_ref, mask_ref, r_in_ref, c_ref, r_ref, home_ref, w_ref, terms_ref, stack_ref):
    iterate_core(pairs, all_ref, mask_ref, r_in_ref, c_ref, r_ref, w_ref, terms_ref, stack_ref)
    part = masked_sum(mask_ref, r_ref)
    n_win, count = home_ref.shape[0], home_ref.shape[1]
    rows_dev = r_ref.shape[1] * LANES // n_win
    lane = lax.broadcasted_iota(jnp.int32, (count, LANES), 1)
    for j in range(n_win):
        b, off = divmod(j * rows_dev, LANES)
        piece = r_ref[:, b, :]
        if off:
            piece = pltpu.roll(piece, LANES - off, 1)
        if off + rows_dev > LANES:
            more = pltpu.roll(r_ref[:, b + 1, :], LANES - off, 1)
            piece = jnp.where(lane < LANES - off, piece, more)
        home_ref[j] = jnp.where(lane < rows_dev, piece, part)


def carry_kernel(lane_id, x_ref, o_ref):
    total = jnp.sum(x_ref[...], axis=0)
    lane = lax.broadcasted_iota(jnp.int32, total.shape, 1)
    row = lax.broadcasted_iota(jnp.int32, total.shape, 0)
    o_ref[...] = jnp.full(o_ref.shape, jnp.sum(jnp.where((lane == lane_id) & (row == 0), total, 0.0)), jnp.float32)


def spectrum_kernel(
    pairs, all_ref, mask_ref, r_in_ref, c_ref, table_ref, o_ref, spread_ref, w_ref, terms_ref, stack_ref
):
    spread = set_weights(pairs, jnp.sum(all_ref[...]) * (1.0 / LANES), mask_ref, r_in_ref, w_ref)

    all_stacks(c_ref, w_ref, terms_ref, stack_ref)
    spread_ref[...] = jnp.full(spread_ref.shape, spread, jnp.float32)
    lane = lax.broadcasted_iota(jnp.int32, (L, LANES), 1)
    stacks = stack_ref[0]
    for s in range(1, c_ref.shape[0]):
        stacks = jnp.where(lane // 16 == s, stack_ref[s], stacks)
    both = jnp.dot(table_ref[...], stacks, precision=HIGHEST, preferred_element_type=jnp.float32)
    freq_count = table_ref.shape[0] // 2
    part = lax.broadcasted_iota(jnp.int32, (freq_count, LANES), 1) % 4
    o_ref[...] = jnp.where(part == 0, both[:freq_count], jnp.where(part == 1, both[freq_count:], 0.0))


def beam_kernel(gain, x_ref, cos_ref, sin_ref, fine_cos_ref, fine_sin_ref, o_ref):
    x = x_ref[...]
    yc = lax.dot_general(x, cos_ref[...], TN, precision=HIGHEST, preferred_element_type=jnp.float32)
    ys = lax.dot_general(x, sin_ref[...], TN, precision=HIGHEST, preferred_element_type=jnp.float32)
    c, s = fine_cos_ref[...], fine_sin_ref[...]
    u = yc * c - ys * s
    v = ys * c + yc * s
    rows = o_ref.shape[1] * 2
    out = lax.broadcasted_iota(jnp.int32, (rows, LANES), 0)
    lane = lax.broadcasted_iota(jnp.int32, (rows, LANES), 1)
    same = lane // 16 == out // 2
    imag, part = out % 2, lane % 4
    pick_u = jnp.where(same & (part == imag), 1.0, 0.0)
    pick_v = jnp.where(same & (part == 0) & (imag == 1), 1.0, 0.0) - jnp.where(
        same & (part == 1) & (imag == 0), 1.0, 0.0
    )
    beams = jnp.dot(pick_u, u, precision=HIGHEST, preferred_element_type=jnp.float32) + jnp.dot(
        pick_v, v, precision=HIGHEST, preferred_element_type=jnp.float32
    )
    for i in range(o_ref.shape[1]):
        o_ref[0, i] = beams[2 * i:2 * i + 2] * gain


def cos_sin(freq_id, chan_ids, slow_count, modulus):
    slow_ids = jnp.arange(slow_count, dtype=jnp.int32) - slow_count // 2
    phase_ids = jnp.mod((freq_id * chan_ids)[:, None] * slow_ids[None, :], modulus)
    angles = 2.0 * math.pi / modulus * phase_ids.astype(jnp.float32)
    return jnp.cos(angles), jnp.sin(angles)


VMEM = pl.BlockSpec(memory_space=pltpu.VMEM)
SMEM = pl.BlockSpec(memory_space=pltpu.SMEM)


def body(spectra, sources, valid):
    win_dev, chan_dev, width = spectra.shape
    freq_count = width // 2
    source_total = sources.shape[0]
    n_win = lax.axis_size("win")
    n_ch = lax.axis_size("ch")
    n_all = n_win * n_ch
    chans = chan_dev * n_ch
    pairs = float(source_total * chans)
    win, ch = lax.axis_index("win"), lax.axis_index("ch")
    y, core = ch // 2, ch % 2
    inverse_np, forward_np = tables(freq_count, L)
    flat = spectra.reshape(win_dev * chan_dev, width)
    rows_dev = win_dev * Q
    rows = n_win * rows_dev
    piece = win_dev * width // LANES
    z_size = 8
    x_size = n_win // z_size

    picked = pl.pallas_call(
        pick_kernel,
        grid_spec=pltpu.PrefetchScalarGridSpec(
            num_scalar_prefetch=1,
            grid=(1,),
            in_specs=[pl.BlockSpec(flat.shape, lambda *_: (0, 0))],
            out_specs=pl.BlockSpec((source_total, piece, LANES), lambda *_: (0, 0, 0)),
        ),
        out_shape=jax.ShapeDtypeStruct((source_total, piece, LANES), jnp.bfloat16),
        name="pick",
    )(sources, flat)
    got = lax.all_to_all(picked, "ch", 0, 0, tiled=True)
    freq_id = win * n_ch + ch
    modulus = 4 * freq_count * P_SIZE
    device = jnp.arange(n_all, dtype=jnp.int32)
    coarse = (device % n_ch) * chan_dev + (device // n_ch) * Q
    cosines, sines = cos_sin(freq_id, coarse, P_SIZE, modulus)
    fine_cos, fine_sin = cos_sin(freq_id, (jnp.arange(LANES, dtype=jnp.int32) // 4) % Q, P_SIZE, modulus)
    got, cosines, sines, fine_cos, fine_sin = lax.optimization_barrier((got, cosines, sines, fine_cos, fine_sin))
    own_mask = valid.astype(jnp.float32)
    mask_lanes = jnp.broadcast_to(own_mask.reshape(win_dev // 4, 1, 4), (win_dev // 4, Q, 4)).reshape(1, rows_dev)
    own = pl.pallas_call(
        own_kernel,
        in_specs=[VMEM, VMEM],
        out_specs=VMEM,
        out_shape=jax.ShapeDtypeStruct((z_size, piece + 8, LANES), jnp.bfloat16),
        compiler_params=PARAMS,
        name="own",
    )(got, jnp.pad(mask_lanes, ((0, 0), (0, LANES - rows_dev))))

    along_z = [[x * z_size + z for z in range(z_size)] for x in range(x_size)]
    own = lax.all_to_all(own, "win", 0, 0, tiled=True, axis_index_groups=along_z)

    def turn_x(d):
        return [(x * z_size + z, (x + d) % x_size * z_size + z) for x in range(x_size) for z in range(z_size)]

    own = jnp.stack([own] + [lax.ppermute(own, "win", turn_x(d)) for d in range(1, x_size)])
    own = own.reshape(n_win, piece + 8, LANES)
    own, own_masks = own[:, :piece], own[:, piece:]

    def turn_y(d):
        return [(i * 2 + c, ((i + d) % 4) * 2 + c) for i in range(n_ch // 2) for c in range(2)]

    with jax.named_scope("along_y"):
        below, above = lax.ppermute(own, "ch", turn_y(1)), lax.ppermute(own, "ch", turn_y(3))
        far = [
            lax.ppermute(below[:n_win // 2], "ch", turn_y(1)),
            lax.ppermute(above[n_win // 2:], "ch", turn_y(3)),
        ]
        mine = jnp.concatenate([own, below] + far + [above]).reshape(4, n_win, piece, LANES)
    with jax.named_scope("cores"):
        theirs = lax.ppermute(mine, "ch", [(i, i ^ 1) for i in range(n_ch)])
    steps = jnp.arange(4, dtype=jnp.int32)
    slot_y = 2 * ((y - steps) % 4)
    ids = jnp.concatenate([slot_y + core, slot_y + 1 - core, (win // z_size)[None]]).astype(jnp.int32)

    with jax.named_scope("main"):
        packed = pl.pallas_call(
            pack_kernel,
            in_specs=[VMEM],
            out_specs=VMEM,
            out_shape=jax.ShapeDtypeStruct((n_win, rows_dev, width), jnp.bfloat16),
            compiler_params=PARAMS,
            name="pack",
        )(flat)
        moved = lax.all_to_all(packed, "win", 0, 0, tiled=True)

    inverse = pltpu.with_memory_space_constraint(jnp.asarray(inverse_np, jnp.bfloat16), pltpu.HBM)
    corr_shape = jax.ShapeDtypeStruct((source_total, L, rows), jnp.bfloat16)
    r_shape = jax.ShapeDtypeStruct((source_total, rows // LANES, LANES), jnp.float32)
    mask_shape = jax.ShapeDtypeStruct((rows // LANES, LANES), jnp.float32)
    part_shape = jax.ShapeDtypeStruct((n_all, LANES), jnp.float32)
    row_weights = pltpu.VMEM(r_shape.shape, jnp.float32)
    terms = pltpu.VMEM((source_total, L + 16, 3 * LANES), jnp.bfloat16)
    stack = pltpu.VMEM((source_total, L, LANES), jnp.float32)
    cross = pltpu.VMEM((rows // 2, width), jnp.bfloat16)
    corr, r, part, mask = pl.pallas_call(
        correlate_kernel,
        in_specs=[SMEM] + [VMEM] * 4 + [pl.BlockSpec(memory_space=pl.ANY)],
        out_specs=[VMEM] * 4,
        out_shape=[corr_shape, r_shape, part_shape, mask_shape],
        scratch_shapes=[
            cross, cross, terms, stack, pltpu.VMEM((L, width), jnp.bfloat16), pltpu.SemaphoreType.DMA
        ],
        compiler_params=PARAMS,
        name="correlate",
    )(ids, moved.reshape(rows, width), mine, theirs, own_masks, inverse)

    parts = lax.all_to_all(part, ("win", "ch"), 0, 0, tiled=True)
    for kernel, shape in (
        (iterate_kernel, part_shape),
        (last_residual_kernel, jax.ShapeDtypeStruct((n_win, source_total, LANES), jnp.float32)),
    ):
        r, part = pl.pallas_call(
            lambda *refs: kernel(pairs, *refs),
            in_specs=[VMEM] * 4,
            out_specs=[VMEM, VMEM],
            out_shape=[r_shape, shape],
            scratch_shapes=[row_weights, terms, stack],
            compiler_params=PARAMS,
            name="iterate",
        )(parts, mask, r, corr)
        if kernel is iterate_kernel:
            parts = lax.all_to_all(part, ("win", "ch"), 0, 0, tiled=True)

    back = lax.all_to_all(part, "win", 0, 0, tiled=True)
    over_win = pl.pallas_call(
        lambda *refs: carry_kernel(rows_dev, *refs),
        in_specs=[VMEM],
        out_specs=VMEM,
        out_shape=jax.ShapeDtypeStruct((n_ch, LANES), jnp.float32),
        compiler_params=PARAMS,
        name="carry",
    )(back)
    parts = lax.all_to_all(over_win, "ch", 0, 0, tiled=True)

    spectrum, spread_sq = pl.pallas_call(
        lambda *refs: spectrum_kernel(pairs, *refs),
        in_specs=[VMEM] * 5,
        out_specs=[VMEM] * 2,
        out_shape=[
            jax.ShapeDtypeStruct((freq_count, LANES), jnp.float32),
            jax.ShapeDtypeStruct((8, LANES), jnp.float32),
        ],
        scratch_shapes=[row_weights, terms, stack],
        compiler_params=PARAMS,
        name="spectrum",
    )(parts, mask, r, corr, jnp.asarray(forward_np))
    pieces = lax.all_to_all(spectrum, ("win", "ch"), 0, 0, tiled=True)

    beamed = pl.pallas_call(
        lambda *refs: beam_kernel(chans ** (-0.5), *refs),
        in_specs=[VMEM] * 5,
        out_specs=VMEM,
        out_shape=jax.ShapeDtypeStruct((1, source_total, 2, P_SIZE), jnp.float32),
        compiler_params=PARAMS,
        name="beam",
    )(pieces, cosines, sines, fine_cos, fine_sin)

    own_mask, back, spread_sq = lax.optimization_barrier((own_mask, back, spread_sq))
    spread_sq = spread_sq[0, 0]
    residual = back[:, :, :rows_dev].reshape(n_win, source_total, win_dev // 4, Q, 4)
    residual = residual.transpose(2, 4, 1, 0, 3).reshape(win_dev, source_total, chan_dev)
    weights = own_mask[:, None, None] * (degrees + 1.0) / (degrees + residual / spread_sq)
    return (weights, beamed)


def solution(mesh):
    return jax.shard_map(
        body,
        mesh=mesh,
        in_specs=(P("win", "ch", None), P(), P("win")),
        out_specs=(P("win", None, "ch"), P(("win", "ch"), None, None, None)),
        check_vma=False,
    )
```

```python
import math

import jax
import jax.numpy as jnp
import numpy as np
from jax import lax
from jax.experimental import pallas as pl
from jax.experimental.pallas import tpu as pltpu
from jax.sharding import PartitionSpec as P

L = 256
P_SIZE = 512
ITERS = 3
Q = 4
LANES = 128
PARAMS = pltpu.CompilerParams(vmem_limit_bytes=16 << 20)

degrees = 3.0
epsilon = 1e-06
HIGHEST = lax.Precision.HIGHEST
NT = (((1,), (1,)), ((), ()))
TN = (((0,), (0,)), ((), ()))


def tables(freq_count, lag_count):
    freq_ids = np.arange(freq_count, dtype=np.int64)
    delays = np.arange(lag_count, dtype=np.int64) - lag_count // 2
    phase_ids = np.mod(freq_ids[:, None] * delays[None, :], 2 * freq_count)
    angles = np.float32(2.0 * math.pi / (2 * freq_count)) * phase_ids.astype(np.float32)
    cosines = np.cos(angles.astype(np.float64)).astype(np.float32)
    sines = np.sin(angles.astype(np.float64)).astype(np.float32)
    inverse_factor = np.float32(1.0 / math.sqrt(freq_count))
    inverse = np.concatenate([cosines * inverse_factor, -sines * inverse_factor], axis=0)
    return np.ascontiguousarray(inverse.T)


def forward_table(freq_count, lag_count):
    freq_ids = jnp.arange(freq_count, dtype=jnp.int32)
    delay_indices = jnp.arange(lag_count, dtype=jnp.int32) - lag_count // 2
    phase_ids = jnp.mod(freq_ids[:, None] * delay_indices[None, :], 2 * freq_count)
    angles = 2.0 * math.pi / (2 * freq_count) * phase_ids.astype(jnp.float32)
    factor = 1.0 / math.sqrt(lag_count)
    return jnp.cos(angles) * factor, -jnp.sin(angles) * factor


def pick_kernel(sources_ref, x_ref, o_ref):
    rows, count = x_ref.shape[0], o_ref.shape[0]
    chan_dev = 128
    row = lax.broadcasted_iota(jnp.int32, (24, rows), 0)
    col = lax.broadcasted_iota(jnp.int32, (24, rows), 1)
    window = (row // 8) * 4 + row % 4
    shift = lax.axis_index("ch") * chan_dev
    blocks = []
    for s in range(count):
        base = sources_ref[s] - shift
        base = jnp.where((base >= 0) & (base < chan_dev), base, -(1 << 20))
        blocks.append(jnp.where(col == window * chan_dev + base, 1.0, 0.0))
    picker = jnp.concatenate(blocks, axis=0).astype(jnp.bfloat16)
    picked = jnp.dot(picker, x_ref[...], preferred_element_type=jnp.float32).reshape(count, 24, 512)
    low = lax.broadcasted_iota(jnp.int32, (8, LANES), 0) < 4
    for s in range(count):
        for t in range(3):
            tile = picked[s, t * 8:(t + 1) * 8, :]
            pair = [
                jnp.where(low, tile[:, p * 256:p * 256 + 128], tile[:, p * 256 + 128:p * 256 + 256])
                for p in range(2)
            ]
            o_ref[s, t * 16:(t + 1) * 16, :] = jnp.concatenate(pair, axis=0).astype(jnp.bfloat16)


def own_kernel(x_ref, mask_ref, o_ref):
    total = x_ref[0].astype(jnp.float32)
    for g in range(1, x_ref.shape[0]):
        total += x_ref[g].astype(jnp.float32)
    rows = total.shape[0]
    masks = jnp.broadcast_to(mask_ref[...], (8, LANES))
    block = jnp.concatenate([total, masks], axis=0).astype(jnp.bfloat16)
    for j in range(o_ref.shape[0]):
        o_ref[j] = block


def pack_kernel(x_ref, o_ref):
    row = lax.broadcasted_iota(jnp.int32, (512, 512), 0)
    col = lax.broadcasted_iota(jnp.int32, (512, 512), 1)
    src = (row % 4) * 128 + (row // 16) * 4 + (row // 4) % 4
    perm = jnp.where(col == src, 1.0, 0.0).astype(jnp.bfloat16)
    for t in range(o_ref.shape[1] // 16):
        got = jnp.dot(perm, x_ref[t * 512:(t + 1) * 512, :], preferred_element_type=jnp.float32)
        o_ref[:, t * 16:(t + 1) * 16, :] = got.astype(jnp.bfloat16).reshape(
            o_ref.shape[0], 16, x_ref.shape[1]
        )


LAG_CHUNK = 64


def three_terms(x):
    high = x.astype(jnp.bfloat16)
    rest = x - high.astype(jnp.float32)
    middle = rest.astype(jnp.bfloat16)
    low = (rest - middle.astype(jnp.float32)).astype(jnp.bfloat16)
    return high, middle, low


def same_channel():
    a = lax.broadcasted_iota(jnp.int32, (3 * LANES, LANES), 0)
    b = lax.broadcasted_iota(jnp.int32, (3 * LANES, LANES), 1)
    return jnp.where((a // 4) % 4 == (b // 4) % 4, 1.0, 0.0).astype(jnp.bfloat16)


def weighted_sums(c_ref, s, w_rows, terms_ref):
    weights = [w_rows[b:b + 1, :] for b in range(w_rows.shape[0])]
    for k in range(L // LAG_CHUNK):
        lags = slice(k * LAG_CHUNK, (k + 1) * LAG_CHUNK)
        acc = jnp.zeros((LAG_CHUNK, LANES), jnp.float32)
        for b, w in enumerate(weights):
            acc += w * c_ref[s, lags, b * LANES:(b + 1) * LANES].astype(jnp.float32)
        for i, term in enumerate(three_terms(acc)):
            terms_ref[s, lags, i * LANES:(i + 1) * LANES] = term
    weight_sum = jnp.broadcast_to(jnp.sum(w_rows[...], axis=0, keepdims=True), (16, LANES))
    for i, term in enumerate(three_terms(weight_sum)):
        terms_ref[s, L:L + 16, i * LANES:(i + 1) * LANES] = term


def finish_stack(terms_ref, s, stack_ref):
    sums = jnp.dot(terms_ref[s], same_channel(), preferred_element_type=jnp.float32)
    stack_ref[s] = sums[:L] * (1.0 / sums[L:L + 1])


def all_stacks(c_ref, w_ref, terms_ref, stack_ref):
    count = c_ref.shape[0]
    for s in range(count):
        weighted_sums(c_ref, s, w_ref.at[s], terms_ref)
        if s:
            finish_stack(terms_ref, s - 1, stack_ref)
    finish_stack(terms_ref, count - 1, stack_ref)


def residuals(c_ref, s, stack_ref, r_ref):
    for b in range(r_ref.shape[1]):
        total = jnp.zeros((8, LANES), jnp.float32)
        for k in range(L // LAG_CHUNK):
            lags = slice(k * LAG_CHUNK, (k + 1) * LAG_CHUNK)
            d = c_ref[s, lags, b * LANES:(b + 1) * LANES].astype(jnp.float32) - stack_ref[s, lags, :]
            total += jnp.sum((d * d).reshape(LAG_CHUNK // 8, 8, LANES), axis=0)
        r_ref[s, b:b + 1, :] = jnp.sum(total, axis=0, keepdims=True) * (1.0 / L)


def masked_sum(mask_ref, r_ref):
    return jnp.sum(mask_ref[...][None] * r_ref[...])


def correlate_kernel(
    ids_ref, a_ref, x_ref, y_ref, masks_ref, inv_hbm, c_ref, r_ref, part_ref, mask_ref, even_ref, odd_ref, terms_ref, stack_ref, inv_ref, sem
):
    table = pltpu.make_async_copy(inv_hbm, inv_ref, sem)
    table.start()
    n_win, rows = x_ref.shape[1], a_ref.shape[0]
    half = a_ref.shape[1] // 2
    rows_dev = rows // n_win
    z_size, x_size = 8, n_win // 8
    far = [(ids_ref[8] - x + x_size) % x_size * z_size for x in range(x_size)]
    low = lax.broadcasted_iota(jnp.int32, (8, LANES), 0) < 4

    lane = lax.broadcasted_iota(jnp.int32, (8, LANES), 1)
    pieces = [jnp.zeros((8, LANES), jnp.float32) for _ in range(rows // LANES)]
    for j in range(n_win):
        row = masks_ref[far[j // z_size] + j % z_size].astype(jnp.float32)
        b, off = divmod(j * rows_dev, LANES)
        turned = pltpu.roll(row, off, 1) if off else row
        end = off + rows_dev
        pieces[b] = jnp.where((lane >= off) & (lane < end), turned, pieces[b])
        if end > LANES:
            pieces[b + 1] = jnp.where(lane < end - LANES, turned, pieces[b + 1])
    for b, piece in enumerate(pieces):
        mask_ref[b:b + 1, :] = piece[0:1, :]

    count, half_rows = c_ref.shape[0], rows // 2
    half_win = n_win // 2

    def fill(cross_ref, s_ref, k, side):
        for j in range(half_win):
            held = far[(side * half_win + j) // z_size] + j % z_size
            for t in range(3):
                quarters = []
                for p in range(2):
                    at = t * 16 + p * 8
                    tile = s_ref[k, held, at:at + 8, :].astype(jnp.float32)
                    turned = pltpu.roll(tile, 4, 0)
                    quarters += [jnp.where(low, tile, turned), jnp.where(low, turned, tile)]
                at = slice(j * rows_dev + t * 16, j * rows_dev + t * 16 + 16)
                src = slice(at.start + side * half_rows, at.stop + side * half_rows)
                for i in range(2):
                    a = jnp.concatenate([quarters[i]] * 2, axis=0)
                    b = jnp.concatenate([quarters[2 + i]] * 2, axis=0)
                    first = slice(i * LANES, (i + 1) * LANES)
                    second = slice(half + i * LANES, half + (i + 1) * LANES)
                    u = a_ref[src, first].astype(jnp.float32)
                    v = a_ref[src, second].astype(jnp.float32)
                    cross_ref[at, first] = (a * u + b * v).astype(jnp.bfloat16)
                    cross_ref[at, second] = (b * u - a * v).astype(jnp.bfloat16)

    def correlate(cross_ref, s, side):
        for n in range(half_rows // 256):
            got = lax.dot_general(
                inv_ref[...], cross_ref[n * 256:(n + 1) * 256, :], NT, preferred_element_type=jnp.float32
            )
            at = side * half_rows + n * 256
            c_ref[s, :, at:at + 256] = got.astype(jnp.bfloat16)

    fill(even_ref, x_ref, 0, 0)
    table.wait()
    pairs_of_slots = count // 2

    def slot(k, carry):
        after = jnp.minimum(k + 1, pairs_of_slots - 1)
        for s, s_ref, next_ref, next_k in (
            (ids_ref[k], x_ref, y_ref, k),
            (ids_ref[pairs_of_slots + k], y_ref, x_ref, after),
        ):
            correlate(even_ref, s, 0)
            fill(odd_ref, s_ref, k, 1)
            correlate(odd_ref, s, 1)
            fill(even_ref, next_ref, next_k, 0)
            weighted_sums(c_ref, s, mask_ref, terms_ref)
            finish_stack(terms_ref, s, stack_ref)
        return carry

    lax.fori_loop(0, pairs_of_slots, slot, 0)

    def last(s, carry):
        residuals(c_ref, s, stack_ref, r_ref)
        return carry

    lax.fori_loop(0, count, last, 0)
    part_ref[...] = jnp.full(part_ref.shape, masked_sum(mask_ref, r_ref), jnp.float32)


def set_weights(pairs, total, mask_ref, r_ref, w_ref):
    mask = mask_ref[...]
    spread = total / (pairs * jnp.sum(mask) * (1.0 / Q)) + epsilon
    w_ref[...] = mask[None] * (degrees + 1.0) / (degrees + r_ref[...] / spread)
    return spread


def iterate_core(pairs, all_ref, mask_ref, r_in_ref, c_ref, r_ref, w_ref, terms_ref, stack_ref):
    set_weights(pairs, jnp.sum(all_ref[...]) * (1.0 / LANES), mask_ref, r_in_ref, w_ref)

    all_stacks(c_ref, w_ref, terms_ref, stack_ref)

    def last(s, carry):
        residuals(c_ref, s, stack_ref, r_ref)
        return carry

    lax.fori_loop(0, c_ref.shape[0], last, 0)


def iterate_kernel(pairs, all_ref, mask_ref, r_in_ref, c_ref, r_ref, part_ref, w_ref, terms_ref, stack_ref):
    iterate_core(pairs, all_ref, mask_ref, r_in_ref, c_ref, r_ref, w_ref, terms_ref, stack_ref)
    part_ref[...] = jnp.full(part_ref.shape, masked_sum(mask_ref, r_ref), jnp.float32)


def last_residual_kernel(pairs, all_ref, mask_ref, r_in_ref, c_ref, r_ref, home_ref, w_ref, terms_ref, stack_ref):
    iterate_core(pairs, all_ref, mask_ref, r_in_ref, c_ref, r_ref, w_ref, terms_ref, stack_ref)
    part = masked_sum(mask_ref, r_ref)
    n_win, count = home_ref.shape[0], home_ref.shape[1]
    rows_dev = r_ref.shape[1] * LANES // n_win
    lane = lax.broadcasted_iota(jnp.int32, (count, LANES), 1)
    for j in range(n_win):
        b, off = divmod(j * rows_dev, LANES)
        piece = r_ref[:, b, :]
        if off:
            piece = pltpu.roll(piece, LANES - off, 1)
        if off + rows_dev > LANES:
            more = pltpu.roll(r_ref[:, b + 1, :], LANES - off, 1)
            piece = jnp.where(lane < LANES - off, piece, more)
        home_ref[j] = jnp.where(lane < rows_dev, piece, part)


def carry_kernel(lane_id, x_ref, o_ref):
    total = jnp.sum(x_ref[...], axis=0)
    lane = lax.broadcasted_iota(jnp.int32, total.shape, 1)
    row = lax.broadcasted_iota(jnp.int32, total.shape, 0)
    o_ref[...] = jnp.full(o_ref.shape, jnp.sum(jnp.where((lane == lane_id) & (row == 0), total, 0.0)), jnp.float32)


def spectrum_kernel(
    pairs, all_ref, mask_ref, r_in_ref, c_ref, cos_ref, sin_ref, o_ref, spread_ref, w_ref, terms_ref, stack_ref
):
    spread = set_weights(pairs, jnp.sum(all_ref[...]) * (1.0 / LANES), mask_ref, r_in_ref, w_ref)

    all_stacks(c_ref, w_ref, terms_ref, stack_ref)
    spread_ref[...] = jnp.full(spread_ref.shape, spread, jnp.float32)
    lane = lax.broadcasted_iota(jnp.int32, (L, LANES), 1)
    stacks = stack_ref[0]
    for s in range(1, c_ref.shape[0]):
        stacks = jnp.where(lane // 16 == s, stack_ref[s], stacks)
    real = jnp.dot(cos_ref[...], stacks, precision=HIGHEST, preferred_element_type=jnp.float32)
    imag = jnp.dot(sin_ref[...], stacks, precision=HIGHEST, preferred_element_type=jnp.float32)
    part = lax.broadcasted_iota(jnp.int32, real.shape, 1) % 4
    o_ref[...] = jnp.where(part == 0, real, jnp.where(part == 1, imag, 0.0))


def beam_kernel(gain, x_ref, cos_ref, sin_ref, fine_cos_ref, fine_sin_ref, o_ref):
    x = x_ref[...]
    yc = lax.dot_general(x, cos_ref[...], TN, precision=HIGHEST, preferred_element_type=jnp.float32)
    ys = lax.dot_general(x, sin_ref[...], TN, precision=HIGHEST, preferred_element_type=jnp.float32)
    c, s = fine_cos_ref[...], fine_sin_ref[...]
    u = yc * c - ys * s
    v = ys * c + yc * s
    rows = o_ref.shape[1] * 2
    out = lax.broadcasted_iota(jnp.int32, (rows, LANES), 0)
    lane = lax.broadcasted_iota(jnp.int32, (rows, LANES), 1)
    same = lane // 16 == out // 2
    imag, part = out % 2, lane % 4
    pick_u = jnp.where(same & (part == imag), 1.0, 0.0)
    pick_v = jnp.where(same & (part == 0) & (imag == 1), 1.0, 0.0) - jnp.where(
        same & (part == 1) & (imag == 0), 1.0, 0.0
    )
    beams = jnp.dot(pick_u, u, precision=HIGHEST, preferred_element_type=jnp.float32) + jnp.dot(
        pick_v, v, precision=HIGHEST, preferred_element_type=jnp.float32
    )
    for i in range(o_ref.shape[1]):
        o_ref[0, i] = beams[2 * i:2 * i + 2] * gain


def cos_sin(freq_id, chan_ids, slow_count, modulus):
    slow_ids = jnp.arange(slow_count, dtype=jnp.int32) - slow_count // 2
    phase_ids = jnp.mod((freq_id * chan_ids)[:, None] * slow_ids[None, :], modulus)
    angles = 2.0 * math.pi / modulus * phase_ids.astype(jnp.float32)
    return jnp.cos(angles), jnp.sin(angles)


VMEM = pl.BlockSpec(memory_space=pltpu.VMEM)
SMEM = pl.BlockSpec(memory_space=pltpu.SMEM)


def body(spectra, sources, valid):
    win_dev, chan_dev, width = spectra.shape
    freq_count = width // 2
    source_total = sources.shape[0]
    n_win = lax.axis_size("win")
    n_ch = lax.axis_size("ch")
    n_all = n_win * n_ch
    chans = chan_dev * n_ch
    pairs = float(source_total * chans)
    win, ch = lax.axis_index("win"), lax.axis_index("ch")
    y, core = ch // 2, ch % 2
    inverse_np = tables(freq_count, L)
    flat = spectra.reshape(win_dev * chan_dev, width)
    rows_dev = win_dev * Q
    rows = n_win * rows_dev
    piece = win_dev * width // LANES
    z_size = 8
    x_size = n_win // z_size

    picked = pl.pallas_call(
        pick_kernel,
        grid_spec=pltpu.PrefetchScalarGridSpec(
            num_scalar_prefetch=1,
            grid=(1,),
            in_specs=[pl.BlockSpec(flat.shape, lambda *_: (0, 0))],
            out_specs=pl.BlockSpec((source_total, piece, LANES), lambda *_: (0, 0, 0)),
        ),
        out_shape=jax.ShapeDtypeStruct((source_total, piece, LANES), jnp.bfloat16),
        name="pick",
    )(sources, flat)
    got = lax.all_to_all(picked, "ch", 0, 0, tiled=True)
    freq_id = win * n_ch + ch
    modulus = 4 * freq_count * P_SIZE
    device = jnp.arange(n_all, dtype=jnp.int32)
    coarse = (device % n_ch) * chan_dev + (device // n_ch) * Q
    cosines, sines = cos_sin(freq_id, coarse, P_SIZE, modulus)
    fine_cos, fine_sin = cos_sin(freq_id, (jnp.arange(LANES, dtype=jnp.int32) // 4) % Q, P_SIZE, modulus)
    got, flat, cosines, sines, fine_cos, fine_sin = lax.optimization_barrier(
        (got, flat, cosines, sines, fine_cos, fine_sin)
    )
    own_mask = valid.astype(jnp.float32)
    mask_lanes = jnp.broadcast_to(own_mask.reshape(win_dev // 4, 1, 4), (win_dev // 4, Q, 4)).reshape(1, rows_dev)
    own = pl.pallas_call(
        own_kernel,
        in_specs=[VMEM, VMEM],
        out_specs=VMEM,
        out_shape=jax.ShapeDtypeStruct((z_size, piece + 8, LANES), jnp.bfloat16),
        compiler_params=PARAMS,
        name="own",
    )(got, jnp.pad(mask_lanes, ((0, 0), (0, LANES - rows_dev))))

    along_z = [[x * z_size + z for z in range(z_size)] for x in range(x_size)]
    own = lax.all_to_all(own, "win", 0, 0, tiled=True, axis_index_groups=along_z)
    forward_cos, forward_sin = forward_table(freq_count, L)

    def turn_x(d):
        return [(x * z_size + z, (x + d) % x_size * z_size + z) for x in range(x_size) for z in range(z_size)]

    own = jnp.stack([own] + [lax.ppermute(own, "win", turn_x(d)) for d in range(1, x_size)])
    own = own.reshape(n_win, piece + 8, LANES)
    own, own_masks = own[:, :piece], own[:, piece:]

    def turn_y(d):
        return [(i * 2 + c, ((i + d) % 4) * 2 + c) for i in range(n_ch // 2) for c in range(2)]

    with jax.named_scope("along_y"):
        below, above = lax.ppermute(own, "ch", turn_y(1)), lax.ppermute(own, "ch", turn_y(3))
        far = [
            lax.ppermute(below[:n_win // 2], "ch", turn_y(1)),
            lax.ppermute(above[n_win // 2:], "ch", turn_y(3)),
        ]
        mine = jnp.concatenate([own, below] + far + [above]).reshape(4, n_win, piece, LANES)
    with jax.named_scope("cores"):
        theirs = lax.ppermute(mine, "ch", [(i, i ^ 1) for i in range(n_ch)])
    steps = jnp.arange(4, dtype=jnp.int32)
    slot_y = 2 * ((y - steps) % 4)
    ids = jnp.concatenate([slot_y + core, slot_y + 1 - core, (win // z_size)[None]]).astype(jnp.int32)

    with jax.named_scope("main"):
        packed = pl.pallas_call(
            pack_kernel,
            in_specs=[VMEM],
            out_specs=VMEM,
            out_shape=jax.ShapeDtypeStruct((n_win, rows_dev, width), jnp.bfloat16),
            compiler_params=PARAMS,
            name="pack",
        )(flat)
        packed, forward_cos, forward_sin = lax.optimization_barrier((packed, forward_cos, forward_sin))
        moved = lax.all_to_all(packed, "win", 0, 0, tiled=True)

    inverse = pltpu.with_memory_space_constraint(jnp.asarray(inverse_np, jnp.bfloat16), pltpu.HBM)
    corr_shape = jax.ShapeDtypeStruct((source_total, L, rows), jnp.bfloat16)
    r_shape = jax.ShapeDtypeStruct((source_total, rows // LANES, LANES), jnp.float32)
    mask_shape = jax.ShapeDtypeStruct((rows // LANES, LANES), jnp.float32)
    part_shape = jax.ShapeDtypeStruct((n_all, LANES), jnp.float32)
    row_weights = pltpu.VMEM(r_shape.shape, jnp.float32)
    terms = pltpu.VMEM((source_total, L + 16, 3 * LANES), jnp.bfloat16)
    stack = pltpu.VMEM((source_total, L, LANES), jnp.float32)
    cross = pltpu.VMEM((rows // 2, width), jnp.bfloat16)
    corr, r, part, mask = pl.pallas_call(
        correlate_kernel,
        in_specs=[SMEM] + [VMEM] * 4 + [pl.BlockSpec(memory_space=pl.ANY)],
        out_specs=[VMEM] * 4,
        out_shape=[corr_shape, r_shape, part_shape, mask_shape],
        scratch_shapes=[
            cross, cross, terms, stack, pltpu.VMEM((L, width), jnp.bfloat16), pltpu.SemaphoreType.DMA
        ],
        compiler_params=PARAMS,
        name="correlate",
    )(ids, moved.reshape(rows, width), mine, theirs, own_masks, inverse)

    parts = lax.all_to_all(part, ("win", "ch"), 0, 0, tiled=True)
    for kernel, shape in (
        (iterate_kernel, part_shape),
        (last_residual_kernel, jax.ShapeDtypeStruct((n_win, source_total, LANES), jnp.float32)),
    ):
        r, part = pl.pallas_call(
            lambda *refs: kernel(pairs, *refs),
            in_specs=[VMEM] * 4,
            out_specs=[VMEM, VMEM],
            out_shape=[r_shape, shape],
            scratch_shapes=[row_weights, terms, stack],
            compiler_params=PARAMS,
            name="iterate",
        )(parts, mask, r, corr)
        if kernel is iterate_kernel:
            parts = lax.all_to_all(part, ("win", "ch"), 0, 0, tiled=True)

    back = lax.all_to_all(part, "win", 0, 0, tiled=True)
    over_win = pl.pallas_call(
        lambda *refs: carry_kernel(rows_dev, *refs),
        in_specs=[VMEM],
        out_specs=VMEM,
        out_shape=jax.ShapeDtypeStruct((n_ch, LANES), jnp.float32),
        compiler_params=PARAMS,
        name="carry",
    )(back)
    parts = lax.all_to_all(over_win, "ch", 0, 0, tiled=True)

    spectrum, spread_sq = pl.pallas_call(
        lambda *refs: spectrum_kernel(pairs, *refs),
        in_specs=[VMEM] * 6,
        out_specs=[VMEM] * 2,
        out_shape=[
            jax.ShapeDtypeStruct((freq_count, LANES), jnp.float32),
            jax.ShapeDtypeStruct((n_win, source_total, rows_dev), jnp.float32),
        ],
        scratch_shapes=[row_weights, terms, stack],
        compiler_params=PARAMS,
        name="spectrum",
    )(parts, mask, r, corr, forward_cos, forward_sin)
    pieces = lax.all_to_all(spectrum, ("win", "ch"), 0, 0, tiled=True)

    beamed = pl.pallas_call(
        lambda *refs: beam_kernel(chans ** (-0.5), *refs),
        in_specs=[VMEM] * 5,
        out_specs=VMEM,
        out_shape=jax.ShapeDtypeStruct((1, source_total, 2, P_SIZE), jnp.float32),
        compiler_params=PARAMS,
        name="beam",
    )(pieces, cosines, sines, fine_cos, fine_sin)

    own_mask, back, spread_sq = lax.optimization_barrier((own_mask, back, spread_sq))
    residual = (back[:, :, :rows_dev] / spread_sq).reshape(n_win, source_total, win_dev // 4, Q, 4)
    residual = residual.transpose(2, 4, 1, 0, 3).reshape(win_dev, source_total, chan_dev)
    weights = own_mask[:, None, None] * (degrees + 1.0) / (degrees + residual)
    return (weights, beamed)


def solution(mesh):
    return jax.shard_map(
        body,
        mesh=mesh,
        in_specs=(P("win", "ch", None), P(), P("win")),
        out_specs=(P("win", None, "ch"), P(("win", "ch"), None, None, None)),
        check_vma=False,
    )
```

```python
import math

import jax
import jax.numpy as jnp
import numpy as np
from jax import lax
from jax.experimental import pallas as pl
from jax.experimental.pallas import tpu as pltpu
from jax.sharding import PartitionSpec as P

L = 256
P_SIZE = 512
ITERS = 3
Q = 4
LANES = 128
PARAMS = pltpu.CompilerParams(vmem_limit_bytes=16 << 20)

degrees = 3.0
epsilon = 1e-06
HIGHEST = lax.Precision.HIGHEST
NT = (((1,), (1,)), ((), ()))
TN = (((0,), (0,)), ((), ()))


def tables(freq_count, lag_count):
    freq_ids = np.arange(freq_count, dtype=np.int64)
    delays = np.arange(lag_count, dtype=np.int64) - lag_count // 2
    phase_ids = np.mod(freq_ids[:, None] * delays[None, :], 2 * freq_count)
    angles = np.float32(2.0 * math.pi / (2 * freq_count)) * phase_ids.astype(np.float32)
    cosines = np.cos(angles.astype(np.float64)).astype(np.float32)
    sines = np.sin(angles.astype(np.float64)).astype(np.float32)
    inverse_factor = np.float32(1.0 / math.sqrt(freq_count))
    inverse = np.concatenate([cosines * inverse_factor, -sines * inverse_factor], axis=0)
    return np.ascontiguousarray(inverse.T)


def forward_table(freq_count, lag_count):
    freq_ids = jnp.arange(freq_count, dtype=jnp.int32)
    delay_indices = jnp.arange(lag_count, dtype=jnp.int32) - lag_count // 2
    phase_ids = jnp.mod(freq_ids[:, None] * delay_indices[None, :], 2 * freq_count)
    angles = 2.0 * math.pi / (2 * freq_count) * phase_ids.astype(jnp.float32)
    factor = 1.0 / math.sqrt(lag_count)
    return jnp.cos(angles) * factor, -jnp.sin(angles) * factor


def pick_kernel(sources_ref, x_ref, o_ref):
    rows, count = x_ref.shape[0], o_ref.shape[0]
    chan_dev = 128
    row = lax.broadcasted_iota(jnp.int32, (24, rows), 0)
    col = lax.broadcasted_iota(jnp.int32, (24, rows), 1)
    window = (row // 8) * 4 + row % 4
    shift = lax.axis_index("ch") * chan_dev
    blocks = []
    for s in range(count):
        base = sources_ref[s] - shift
        base = jnp.where((base >= 0) & (base < chan_dev), base, -(1 << 20))
        blocks.append(jnp.where(col == window * chan_dev + base, 1.0, 0.0))
    picker = jnp.concatenate(blocks, axis=0).astype(jnp.bfloat16)
    picked = jnp.dot(picker, x_ref[...], preferred_element_type=jnp.float32).reshape(count, 24, 512)
    low = lax.broadcasted_iota(jnp.int32, (8, LANES), 0) < 4
    for s in range(count):
        for t in range(3):
            tile = picked[s, t * 8:(t + 1) * 8, :]
            pair = [
                jnp.where(low, tile[:, p * 256:p * 256 + 128], tile[:, p * 256 + 128:p * 256 + 256])
                for p in range(2)
            ]
            o_ref[s, t * 16:(t + 1) * 16, :] = jnp.concatenate(pair, axis=0).astype(jnp.bfloat16)


def own_kernel(x_ref, mask_ref, o_ref):
    total = x_ref[0].astype(jnp.float32)
    for g in range(1, x_ref.shape[0]):
        total += x_ref[g].astype(jnp.float32)
    rows = total.shape[0]
    masks = jnp.broadcast_to(mask_ref[...], (8, LANES))
    block = jnp.concatenate([total, masks], axis=0).astype(jnp.bfloat16)
    for j in range(o_ref.shape[0]):
        o_ref[j] = block


def pack_kernel(x_ref, o_ref):
    row = lax.broadcasted_iota(jnp.int32, (512, 512), 0)
    col = lax.broadcasted_iota(jnp.int32, (512, 512), 1)
    src = (row % 4) * 128 + (row // 16) * 4 + (row // 4) % 4
    perm = jnp.where(col == src, 1.0, 0.0).astype(jnp.bfloat16)
    for t in range(o_ref.shape[1] // 16):
        got = jnp.dot(perm, x_ref[t * 512:(t + 1) * 512, :], preferred_element_type=jnp.float32)
        o_ref[:, t * 16:(t + 1) * 16, :] = got.astype(jnp.bfloat16).reshape(
            o_ref.shape[0], 16, x_ref.shape[1]
        )


LAG_CHUNK = 64


def three_terms(x):
    high = x.astype(jnp.bfloat16)
    rest = x - high.astype(jnp.float32)
    middle = rest.astype(jnp.bfloat16)
    low = (rest - middle.astype(jnp.float32)).astype(jnp.bfloat16)
    return high, middle, low


def same_channel():
    a = lax.broadcasted_iota(jnp.int32, (3 * LANES, LANES), 0)
    b = lax.broadcasted_iota(jnp.int32, (3 * LANES, LANES), 1)
    return jnp.where((a // 4) % 4 == (b // 4) % 4, 1.0, 0.0).astype(jnp.bfloat16)


def weighted_sums(c_ref, s, w_rows, terms_ref):
    weights = [w_rows[b:b + 1, :] for b in range(w_rows.shape[0])]
    for k in range(L // LAG_CHUNK):
        lags = slice(k * LAG_CHUNK, (k + 1) * LAG_CHUNK)
        acc = jnp.zeros((LAG_CHUNK, LANES), jnp.float32)
        for b, w in enumerate(weights):
            acc += w * c_ref[s, lags, b * LANES:(b + 1) * LANES].astype(jnp.float32)
        for i, term in enumerate(three_terms(acc)):
            terms_ref[s, lags, i * LANES:(i + 1) * LANES] = term
    weight_sum = jnp.broadcast_to(jnp.sum(w_rows[...], axis=0, keepdims=True), (16, LANES))
    for i, term in enumerate(three_terms(weight_sum)):
        terms_ref[s, L:L + 16, i * LANES:(i + 1) * LANES] = term


def finish_stack(terms_ref, s, stack_ref):
    sums = jnp.dot(terms_ref[s], same_channel(), preferred_element_type=jnp.float32)
    stack_ref[s] = sums[:L] * (1.0 / sums[L:L + 1])


def all_stacks(c_ref, w_ref, terms_ref, stack_ref):
    count = c_ref.shape[0]
    for s in range(count):
        weighted_sums(c_ref, s, w_ref.at[s], terms_ref)
        if s:
            finish_stack(terms_ref, s - 1, stack_ref)
    finish_stack(terms_ref, count - 1, stack_ref)


def residuals(c_ref, s, stack_ref, r_ref):
    for b in range(r_ref.shape[1]):
        total = jnp.zeros((8, LANES), jnp.float32)
        for k in range(L // LAG_CHUNK):
            lags = slice(k * LAG_CHUNK, (k + 1) * LAG_CHUNK)
            d = c_ref[s, lags, b * LANES:(b + 1) * LANES].astype(jnp.float32) - stack_ref[s, lags, :]
            total += jnp.sum((d * d).reshape(LAG_CHUNK // 8, 8, LANES), axis=0)
        r_ref[s, b:b + 1, :] = jnp.sum(total, axis=0, keepdims=True) * (1.0 / L)


def masked_sum(mask_ref, r_ref):
    return jnp.sum(mask_ref[...][None] * r_ref[...])


def correlate_kernel(
    ids_ref, a_ref, x_ref, y_hbm, masks_ref, inv_hbm, c_ref, r_ref, part_ref, mask_ref, even_ref, odd_ref, terms_ref, stack_ref, inv_ref, y_ref, sem, y_sem
):
    table = pltpu.make_async_copy(inv_hbm, inv_ref, sem)
    table.start()
    others = pltpu.make_async_copy(y_hbm, y_ref, y_sem)
    others.start()
    n_win, rows = x_ref.shape[1], a_ref.shape[0]
    half = a_ref.shape[1] // 2
    rows_dev = rows // n_win
    z_size, x_size = 8, n_win // 8
    far = [(ids_ref[8] - x + x_size) % x_size * z_size for x in range(x_size)]
    low = lax.broadcasted_iota(jnp.int32, (8, LANES), 0) < 4

    lane = lax.broadcasted_iota(jnp.int32, (8, LANES), 1)
    pieces = [jnp.zeros((8, LANES), jnp.float32) for _ in range(rows // LANES)]
    for j in range(n_win):
        row = masks_ref[far[j // z_size] + j % z_size].astype(jnp.float32)
        b, off = divmod(j * rows_dev, LANES)
        turned = pltpu.roll(row, off, 1) if off else row
        end = off + rows_dev
        pieces[b] = jnp.where((lane >= off) & (lane < end), turned, pieces[b])
        if end > LANES:
            pieces[b + 1] = jnp.where(lane < end - LANES, turned, pieces[b + 1])
    for b, piece in enumerate(pieces):
        mask_ref[b:b + 1, :] = piece[0:1, :]

    count, half_rows = c_ref.shape[0], rows // 2
    half_win = n_win // 2

    def fill(cross_ref, s_ref, k, side):
        for j in range(half_win):
            held = far[(side * half_win + j) // z_size] + j % z_size
            for t in range(3):
                quarters = []
                for p in range(2):
                    at = t * 16 + p * 8
                    tile = s_ref[k, held, at:at + 8, :].astype(jnp.float32)
                    turned = pltpu.roll(tile, 4, 0)
                    quarters += [jnp.where(low, tile, turned), jnp.where(low, turned, tile)]
                at = slice(j * rows_dev + t * 16, j * rows_dev + t * 16 + 16)
                src = slice(at.start + side * half_rows, at.stop + side * half_rows)
                for i in range(2):
                    a = jnp.concatenate([quarters[i]] * 2, axis=0)
                    b = jnp.concatenate([quarters[2 + i]] * 2, axis=0)
                    first = slice(i * LANES, (i + 1) * LANES)
                    second = slice(half + i * LANES, half + (i + 1) * LANES)
                    u = a_ref[src, first].astype(jnp.float32)
                    v = a_ref[src, second].astype(jnp.float32)
                    cross_ref[at, first] = (a * u + b * v).astype(jnp.bfloat16)
                    cross_ref[at, second] = (b * u - a * v).astype(jnp.bfloat16)

    def correlate(cross_ref, s, side):
        for n in range(half_rows // 256):
            got = lax.dot_general(
                inv_ref[...], cross_ref[n * 256:(n + 1) * 256, :], NT, preferred_element_type=jnp.float32
            )
            at = side * half_rows + n * 256
            c_ref[s, :, at:at + 256] = got.astype(jnp.bfloat16)

    fill(even_ref, x_ref, 0, 0)
    table.wait()
    others.wait()
    pairs_of_slots = count // 2

    def slot(k, carry):
        after = jnp.minimum(k + 1, pairs_of_slots - 1)
        for s, s_ref, next_ref, next_k in (
            (ids_ref[k], x_ref, y_ref, k),
            (ids_ref[pairs_of_slots + k], y_ref, x_ref, after),
        ):
            correlate(even_ref, s, 0)
            fill(odd_ref, s_ref, k, 1)
            correlate(odd_ref, s, 1)
            fill(even_ref, next_ref, next_k, 0)
            weighted_sums(c_ref, s, mask_ref, terms_ref)
            finish_stack(terms_ref, s, stack_ref)
        return carry

    lax.fori_loop(0, pairs_of_slots, slot, 0)

    def last(s, carry):
        residuals(c_ref, s, stack_ref, r_ref)
        return carry

    lax.fori_loop(0, count, last, 0)
    part_ref[...] = jnp.full(part_ref.shape, masked_sum(mask_ref, r_ref), jnp.float32)


def set_weights(pairs, total, mask_ref, r_ref, w_ref):
    mask = mask_ref[...]
    spread = total / (pairs * jnp.sum(mask) * (1.0 / Q)) + epsilon
    w_ref[...] = mask[None] * (degrees + 1.0) / (degrees + r_ref[...] / spread)
    return spread


def iterate_core(pairs, all_ref, mask_ref, r_in_ref, c_ref, r_ref, w_ref, terms_ref, stack_ref):
    set_weights(pairs, jnp.sum(all_ref[...]) * (1.0 / LANES), mask_ref, r_in_ref, w_ref)

    all_stacks(c_ref, w_ref, terms_ref, stack_ref)

    def last(s, carry):
        residuals(c_ref, s, stack_ref, r_ref)
        return carry

    lax.fori_loop(0, c_ref.shape[0], last, 0)


def iterate_kernel(pairs, all_ref, mask_ref, r_in_ref, c_ref, r_ref, part_ref, w_ref, terms_ref, stack_ref):
    iterate_core(pairs, all_ref, mask_ref, r_in_ref, c_ref, r_ref, w_ref, terms_ref, stack_ref)
    part_ref[...] = jnp.full(part_ref.shape, masked_sum(mask_ref, r_ref), jnp.float32)


def last_residual_kernel(pairs, all_ref, mask_ref, r_in_ref, c_ref, r_ref, home_ref, w_ref, terms_ref, stack_ref):
    iterate_core(pairs, all_ref, mask_ref, r_in_ref, c_ref, r_ref, w_ref, terms_ref, stack_ref)
    part = masked_sum(mask_ref, r_ref)
    n_win, count = home_ref.shape[0], home_ref.shape[1]
    rows_dev = r_ref.shape[1] * LANES // n_win
    lane = lax.broadcasted_iota(jnp.int32, (count, LANES), 1)
    for j in range(n_win):
        b, off = divmod(j * rows_dev, LANES)
        piece = r_ref[:, b, :]
        if off:
            piece = pltpu.roll(piece, LANES - off, 1)
        if off + rows_dev > LANES:
            more = pltpu.roll(r_ref[:, b + 1, :], LANES - off, 1)
            piece = jnp.where(lane < LANES - off, piece, more)
        home_ref[j] = jnp.where(lane < rows_dev, piece, part)


def carry_kernel(lane_id, x_ref, o_ref):
    total = jnp.sum(x_ref[...], axis=0)
    lane = lax.broadcasted_iota(jnp.int32, total.shape, 1)
    row = lax.broadcasted_iota(jnp.int32, total.shape, 0)
    o_ref[...] = jnp.full(o_ref.shape, jnp.sum(jnp.where((lane == lane_id) & (row == 0), total, 0.0)), jnp.float32)


def spectrum_kernel(
    pairs, all_ref, mask_ref, r_in_ref, c_ref, cos_ref, sin_ref, o_ref, spread_ref, w_ref, terms_ref, stack_ref
):
    spread = set_weights(pairs, jnp.sum(all_ref[...]) * (1.0 / LANES), mask_ref, r_in_ref, w_ref)

    all_stacks(c_ref, w_ref, terms_ref, stack_ref)
    spread_ref[...] = jnp.full(spread_ref.shape, spread, jnp.float32)
    lane = lax.broadcasted_iota(jnp.int32, (L, LANES), 1)
    stacks = stack_ref[0]
    for s in range(1, c_ref.shape[0]):
        stacks = jnp.where(lane // 16 == s, stack_ref[s], stacks)
    real = jnp.dot(cos_ref[...], stacks, precision=HIGHEST, preferred_element_type=jnp.float32)
    imag = jnp.dot(sin_ref[...], stacks, precision=HIGHEST, preferred_element_type=jnp.float32)
    part = lax.broadcasted_iota(jnp.int32, real.shape, 1) % 4
    o_ref[...] = jnp.where(part == 0, real, jnp.where(part == 1, imag, 0.0))


def beam_kernel(gain, x_ref, cos_ref, sin_ref, fine_cos_ref, fine_sin_ref, o_ref):
    x = x_ref[...]
    yc = lax.dot_general(x, cos_ref[...], TN, precision=HIGHEST, preferred_element_type=jnp.float32)
    ys = lax.dot_general(x, sin_ref[...], TN, precision=HIGHEST, preferred_element_type=jnp.float32)
    c, s = fine_cos_ref[...], fine_sin_ref[...]
    u = yc * c - ys * s
    v = ys * c + yc * s
    rows = o_ref.shape[1] * 2
    out = lax.broadcasted_iota(jnp.int32, (rows, LANES), 0)
    lane = lax.broadcasted_iota(jnp.int32, (rows, LANES), 1)
    same = lane // 16 == out // 2
    imag, part = out % 2, lane % 4
    pick_u = jnp.where(same & (part == imag), 1.0, 0.0)
    pick_v = jnp.where(same & (part == 0) & (imag == 1), 1.0, 0.0) - jnp.where(
        same & (part == 1) & (imag == 0), 1.0, 0.0
    )
    beams = jnp.dot(pick_u, u, precision=HIGHEST, preferred_element_type=jnp.float32) + jnp.dot(
        pick_v, v, precision=HIGHEST, preferred_element_type=jnp.float32
    )
    for i in range(o_ref.shape[1]):
        o_ref[0, i] = beams[2 * i:2 * i + 2] * gain


def cos_sin(freq_id, chan_ids, slow_count, modulus):
    slow_ids = jnp.arange(slow_count, dtype=jnp.int32) - slow_count // 2
    phase_ids = jnp.mod((freq_id * chan_ids)[:, None] * slow_ids[None, :], modulus)
    angles = 2.0 * math.pi / modulus * phase_ids.astype(jnp.float32)
    return jnp.cos(angles), jnp.sin(angles)


VMEM = pl.BlockSpec(memory_space=pltpu.VMEM)
SMEM = pl.BlockSpec(memory_space=pltpu.SMEM)


def body(spectra, sources, valid):
    win_dev, chan_dev, width = spectra.shape
    freq_count = width // 2
    source_total = sources.shape[0]
    n_win = lax.axis_size("win")
    n_ch = lax.axis_size("ch")
    n_all = n_win * n_ch
    chans = chan_dev * n_ch
    pairs = float(source_total * chans)
    win, ch = lax.axis_index("win"), lax.axis_index("ch")
    y, core = ch // 2, ch % 2
    inverse_np = tables(freq_count, L)
    flat = spectra.reshape(win_dev * chan_dev, width)
    rows_dev = win_dev * Q
    rows = n_win * rows_dev
    piece = win_dev * width // LANES
    z_size = 8
    x_size = n_win // z_size

    picked = pl.pallas_call(
        pick_kernel,
        grid_spec=pltpu.PrefetchScalarGridSpec(
            num_scalar_prefetch=1,
            grid=(1,),
            in_specs=[pl.BlockSpec(flat.shape, lambda *_: (0, 0))],
            out_specs=pl.BlockSpec((source_total, piece, LANES), lambda *_: (0, 0, 0)),
        ),
        out_shape=jax.ShapeDtypeStruct((source_total, piece, LANES), jnp.bfloat16),
        name="pick",
    )(sources, flat)
    got = lax.all_to_all(picked, "ch", 0, 0, tiled=True)
    freq_id = win * n_ch + ch
    modulus = 4 * freq_count * P_SIZE
    device = jnp.arange(n_all, dtype=jnp.int32)
    coarse = (device % n_ch) * chan_dev + (device // n_ch) * Q
    cosines, sines = cos_sin(freq_id, coarse, P_SIZE, modulus)
    fine_cos, fine_sin = cos_sin(freq_id, (jnp.arange(LANES, dtype=jnp.int32) // 4) % Q, P_SIZE, modulus)
    got, flat, cosines, sines, fine_cos, fine_sin = lax.optimization_barrier(
        (got, flat, cosines, sines, fine_cos, fine_sin)
    )
    own_mask = valid.astype(jnp.float32)
    mask_lanes = jnp.broadcast_to(own_mask.reshape(win_dev // 4, 1, 4), (win_dev // 4, Q, 4)).reshape(1, rows_dev)
    own = pl.pallas_call(
        own_kernel,
        in_specs=[VMEM, VMEM],
        out_specs=VMEM,
        out_shape=jax.ShapeDtypeStruct((z_size, piece + 8, LANES), jnp.bfloat16),
        compiler_params=PARAMS,
        name="own",
    )(got, jnp.pad(mask_lanes, ((0, 0), (0, LANES - rows_dev))))

    along_z = [[x * z_size + z for z in range(z_size)] for x in range(x_size)]
    own = lax.all_to_all(own, "win", 0, 0, tiled=True, axis_index_groups=along_z)
    forward_cos, forward_sin = forward_table(freq_count, L)

    def turn_x(d):
        return [(x * z_size + z, (x + d) % x_size * z_size + z) for x in range(x_size) for z in range(z_size)]

    own = jnp.stack([own] + [lax.ppermute(own, "win", turn_x(d)) for d in range(1, x_size)])
    own = own.reshape(n_win, piece + 8, LANES)
    own, own_masks = own[:, :piece], own[:, piece:]

    def turn_y(d):
        return [(i * 2 + c, ((i + d) % 4) * 2 + c) for i in range(n_ch // 2) for c in range(2)]

    with jax.named_scope("along_y"):
        below, above = lax.ppermute(own, "ch", turn_y(1)), lax.ppermute(own, "ch", turn_y(3))
        far = [
            lax.ppermute(below[:n_win // 2], "ch", turn_y(1)),
            lax.ppermute(above[n_win // 2:], "ch", turn_y(3)),
        ]
        mine = jnp.concatenate([own, below] + far + [above]).reshape(4, n_win, piece, LANES)
    with jax.named_scope("cores"):
        theirs = lax.ppermute(mine, "ch", [(i, i ^ 1) for i in range(n_ch)])
    steps = jnp.arange(4, dtype=jnp.int32)
    slot_y = 2 * ((y - steps) % 4)
    ids = jnp.concatenate([slot_y + core, slot_y + 1 - core, (win // z_size)[None]]).astype(jnp.int32)

    with jax.named_scope("main"):
        packed = pl.pallas_call(
            pack_kernel,
            in_specs=[VMEM],
            out_specs=VMEM,
            out_shape=jax.ShapeDtypeStruct((n_win, rows_dev, width), jnp.bfloat16),
            compiler_params=PARAMS,
            name="pack",
        )(flat)
        packed, forward_cos, forward_sin = lax.optimization_barrier((packed, forward_cos, forward_sin))
        moved = lax.all_to_all(packed, "win", 0, 0, tiled=True)

    inverse = pltpu.with_memory_space_constraint(jnp.asarray(inverse_np, jnp.bfloat16), pltpu.HBM)
    corr_shape = jax.ShapeDtypeStruct((source_total, L, rows), jnp.bfloat16)
    r_shape = jax.ShapeDtypeStruct((source_total, rows // LANES, LANES), jnp.float32)
    mask_shape = jax.ShapeDtypeStruct((rows // LANES, LANES), jnp.float32)
    part_shape = jax.ShapeDtypeStruct((n_all, LANES), jnp.float32)
    row_weights = pltpu.VMEM(r_shape.shape, jnp.float32)
    terms = pltpu.VMEM((source_total, L + 16, 3 * LANES), jnp.bfloat16)
    stack = pltpu.VMEM((source_total, L, LANES), jnp.float32)
    cross = pltpu.VMEM((rows // 2, width), jnp.bfloat16)
    corr, r, part, mask = pl.pallas_call(
        correlate_kernel,
        in_specs=[SMEM, VMEM, VMEM, pl.BlockSpec(memory_space=pl.ANY), VMEM, pl.BlockSpec(memory_space=pl.ANY)],
        out_specs=[VMEM] * 4,
        out_shape=[corr_shape, r_shape, part_shape, mask_shape],
        scratch_shapes=[
            cross, cross, terms, stack, pltpu.VMEM((L, width), jnp.bfloat16),
            pltpu.VMEM((4, n_win, piece, LANES), jnp.bfloat16), pltpu.SemaphoreType.DMA, pltpu.SemaphoreType.DMA
        ],
        compiler_params=PARAMS,
        name="correlate",
    )(ids, moved.reshape(rows, width), mine, theirs, own_masks, inverse)

    parts = lax.all_to_all(part, ("win", "ch"), 0, 0, tiled=True)
    for kernel, shape in (
        (iterate_kernel, part_shape),
        (last_residual_kernel, jax.ShapeDtypeStruct((n_win, source_total, LANES), jnp.float32)),
    ):
        r, part = pl.pallas_call(
            lambda *refs: kernel(pairs, *refs),
            in_specs=[VMEM] * 4,
            out_specs=[VMEM, VMEM],
            out_shape=[r_shape, shape],
            scratch_shapes=[row_weights, terms, stack],
            compiler_params=PARAMS,
            name="iterate",
        )(parts, mask, r, corr)
        if kernel is iterate_kernel:
            parts = lax.all_to_all(part, ("win", "ch"), 0, 0, tiled=True)

    back = lax.all_to_all(part, "win", 0, 0, tiled=True)
    over_win = pl.pallas_call(
        lambda *refs: carry_kernel(rows_dev, *refs),
        in_specs=[VMEM],
        out_specs=VMEM,
        out_shape=jax.ShapeDtypeStruct((n_ch, LANES), jnp.float32),
        compiler_params=PARAMS,
        name="carry",
    )(back)
    parts = lax.all_to_all(over_win, "ch", 0, 0, tiled=True)

    spectrum, spread_sq = pl.pallas_call(
        lambda *refs: spectrum_kernel(pairs, *refs),
        in_specs=[VMEM] * 6,
        out_specs=[VMEM] * 2,
        out_shape=[
            jax.ShapeDtypeStruct((freq_count, LANES), jnp.float32),
            jax.ShapeDtypeStruct((n_win, source_total, rows_dev), jnp.float32),
        ],
        scratch_shapes=[row_weights, terms, stack],
        compiler_params=PARAMS,
        name="spectrum",
    )(parts, mask, r, corr, forward_cos, forward_sin)
    pieces = lax.all_to_all(spectrum, ("win", "ch"), 0, 0, tiled=True)

    beamed = pl.pallas_call(
        lambda *refs: beam_kernel(chans ** (-0.5), *refs),
        in_specs=[VMEM] * 5,
        out_specs=VMEM,
        out_shape=jax.ShapeDtypeStruct((1, source_total, 2, P_SIZE), jnp.float32),
        compiler_params=PARAMS,
        name="beam",
    )(pieces, cosines, sines, fine_cos, fine_sin)

    own_mask, back, spread_sq = lax.optimization_barrier((own_mask, back, spread_sq))
    residual = (back[:, :, :rows_dev] / spread_sq).reshape(n_win, source_total, win_dev // 4, Q, 4)
    residual = residual.transpose(2, 4, 1, 0, 3).reshape(win_dev, source_total, chan_dev)
    weights = own_mask[:, None, None] * (degrees + 1.0) / (degrees + residual)
    return (weights, beamed)


def solution(mesh):
    return jax.shard_map(
        body,
        mesh=mesh,
        in_specs=(P("win", "ch", None), P(), P("win")),
        out_specs=(P("win", None, "ch"), P(("win", "ch"), None, None, None)),
        check_vma=False,
    )
```
